32 devices in a mesh: blk: 16 (over z, x, core), feat: 2 (over y).
Axes of the slice: x: 2, y: 2, z: 4, core: 2. Of those that a mesh axis runs over, the one named last changes fastest.
Arguments:
- inputs: bfloat16 [4096, 1024], P('blk'), may hold values from -6 to 6
- col_mask: int32 [2, 1024], replicated, may hold values 0 or 1
- row_mask: int32 [4096], P('blk'), may hold values from 0 to 1
- width_class: int32 [4096], P('blk'), may hold values from 0 to 1
- frequencies: bfloat16 [2048, 2048], P(None, 'feat'), may hold values from -0.375 to 0.375
- phases: float32 [2048], P('feat'), may hold values from -3.140625 to 3.140625
- targets: float32 [4096], P('blk'), may hold values from -6 to 6
- prior_draws: float32 [4096, 16], P('blk'), may hold values from -6 to 6
- hidden_weight: float32 [1024, 2048], P('blk', 'feat'), may hold values from -0.1875 to 0.1875
- hidden_moment: float32 [1024, 2048], P('blk', 'feat'), may hold values from -9.536743e-06 to 9.536743e-06
- hidden_second: float32 [1024, 2048], P('blk', 'feat'), may hold values from 4.2e-14 to 1.7e-13
- alpha_weight: float32 [4096, 16], P('blk'), may hold values from -1.5 to 1.5
- alpha_moment: float32 [4096, 16], P('blk'), may hold values from -2.2888184e-05 to 2.2888184e-05
- alpha_second: float32 [4096, 16], P('blk'), may hold values from 1.7578125e-13 to 7.080078e-13
Outputs:
- norm_before: float32 [], replicated
- resid_norm: float32 [], replicated
- hidden_out: float32 [1024, 2048], P('blk', 'feat')
- hidden_moment_out: float32 [1024, 2048], P('blk', 'feat')
- hidden_second_out: float32 [1024, 2048], P('blk', 'feat')
- hidden_copy: bfloat16 [1024, 2048], P('blk', 'feat')
- alpha_out: float32 [4096, 16], P('blk')
- alpha_moment_out: float32 [4096, 16], P('blk')
- alpha_second_out: float32 [4096, 16], P('blk')
- alpha_copy: bfloat16 [4096, 16], P('blk')
The draws below stay inside these ranges and needn't reach their ends.
All inputs are finite; a program needn't handle non-finite values.
Results may differ from the reference program's by a relative error of at most 0.0034.
Values may be sent and summed in bfloat16 or wider, within the bound.
No kernel may reach another device: no remote copies, remote signals or barrier semaphores. Data moves between devices by JAX's collectives and lax.ppermute only.
A program may use at most 192 MiB of HBM per device.

```python
import math
import jax
import jax.numpy as jnp
from jax import lax

DIN = 1024
H = 2048
F = 2048
S = 16
CLASSES = 2
ADAM_STEP = 10
TOKENS = 4096


def draw_row_mask(key, part):
    position = jnp.arange(TOKENS, dtype=jnp.int32)
    ticket = jax.random.randint(key, (TOKENS,), 0, 4 * TOKENS, dtype=jnp.int32)
    return (ticket < TOKENS + 3 * position).astype(jnp.int32)


def touch_ends(drawn, own_key, low, largest):
    longest = drawn.shape.index(max(drawn.shape))
    spots = []
    for shift in (0, 1):
        where = [jax.random.randint(jax.random.fold_in(own_key, axis), (), 0, length) for axis, length in enumerate(drawn.shape)]
        where[longest] = (where[longest] + shift) % drawn.shape[longest]
        spots.append(tuple(where))
    return drawn.at[spots[0]].set(low).at[spots[1]].set(largest)


def raised(values, rng, source, target, shards_of, factor):
    owner, partner = [(jnp.arange(values.shape[dim]) // (values.shape[dim] // shards_of)).reshape([-1 if axis == dim else 1 for axis in range(values.ndim)]) for dim in (source, target)]
    chosen = jax.random.permutation(rng, shards_of)[partner]
    strong = (owner == chosen) | (owner == (partner + shards_of // 2) % shards_of)
    return jnp.where(strong, factor * values, values)


def block_levels(rng, dims, cuts, low, top_value):
    def one(dim, parts):
        heights = jax.random.uniform(jax.random.fold_in(jax.random.fold_in(rng, 6), dim), (parts,), jnp.float32, low / len(cuts), top_value / len(cuts))
        return jnp.repeat(jnp.exp(heights), dims[dim] // parts).reshape((-1,) + (1,) * (len(dims) - dim - 1))

    factor_of = one(*cuts[0])
    for cut in cuts[1:]:
        factor_of = factor_of * one(*cut)
    return factor_of


def centred(own_key, extent, deviation, bound, shards=(), held_as=jnp.bfloat16):
    loudness = block_levels(own_key, extent, shards, -0.22, 0.18) if shards else 1.0
    drawn = jax.random.normal(own_key, extent, jnp.float32) * deviation * loudness
    return jnp.minimum(jnp.maximum(drawn, -bound), bound).astype(held_as)


def gaussian_with(stream_key, dims, scale, limit, pieces, heavy, kind=jnp.bfloat16):
    values = scale * jax.random.normal(stream_key, dims, jnp.float32)
    if pieces:
        values = values * block_levels(stream_key, dims, pieces, -0.22, 0.18)
    return jnp.clip(raised(values, jax.random.fold_in(stream_key, 3), *heavy), -limit, limit).astype(kind)


def setup_inputs(seed: int = 0) -> dict:
    key_of = jax.random.split(jax.random.key(seed), 15)
    return {
        "inputs": gaussian_with(key_of[0], (TOKENS, DIN), 1.0, 6.0, ((0, 16),), (0, 1, 16, 2.0)),
        "col_mask": touch_ends((jax.random.randint(key_of[1], (CLASSES, DIN), 0, 4) < 3).astype(jnp.int32), jax.random.fold_in(key_of[1], 1), 0, 1),
        "row_mask": draw_row_mask(jax.random.fold_in(key_of[14], 71), 0),
        "width_class": touch_ends(jax.random.randint(key_of[3], (TOKENS,), 0, CLASSES), jax.random.fold_in(key_of[3], 1), 0, CLASSES - 1).astype(jnp.int32),
        "frequencies": centred(key_of[4], (H, F), (H // 8) ** -0.5, 0.375, ((1, 2),)),
        "phases": jnp.clip(jax.random.uniform(key_of[5], (F,), jnp.float32, -3.140625, 3.140625), -3.140625, 3.140625),
        "targets": centred(key_of[6], (TOKENS,), 1.0, 6.0, ((0, 16),), jnp.float32),
        "prior_draws": centred(key_of[7], (TOKENS, S), 1.0, 6.0, ((0, 16),), jnp.float32),
        "hidden_weight": centred(key_of[8], (DIN, H), DIN ** -0.5, 0.1875, ((0, 16), (1, 2)), jnp.float32),
        "hidden_moment": centred(key_of[9], (DIN, H), (7e-7), 9.5367431640625e-06, ((0, 16), (1, 2)), jnp.float32),
        "hidden_second": jnp.clip(jnp.exp(math.log(1.700000004049157e-13) - 1.39812882 * jax.random.uniform(key_of[10], (DIN, H), jnp.float32) ** block_levels(key_of[10], (DIN, H), ((0, 16), (1, 2)), -0.2, 0.2)), 4.19999999405965e-14, 1.700000004049157e-13),
        "alpha_weight": centred(key_of[11], (TOKENS, S), 0.1, 1.5, ((0, 16),), jnp.float32),
        "alpha_moment": centred(key_of[12], (TOKENS, S), (0.11 * 8.5e-4 / TOKENS ** 0.5), 2.288818359375e-05, ((0, 16),), jnp.float32),
        "alpha_second": jnp.clip(jnp.exp(math.log(7.080078168707205e-13) - 1.3932148 * jax.random.uniform(key_of[13], (TOKENS, S), jnp.float32) ** block_levels(key_of[13], (TOKENS, S), ((0, 16),), -0.2, 0.2)), 1.7578125099167868e-13, 7.080078168707205e-13),
    }


PRECISE = lax.Precision.HIGHEST
NOISE = 0.01
CLIP_AT = 0.01
BETA_ONE = 0.9
BETA_TWO = 0.999
ADAM_EPS = 1e-08
DECAY = 0.01

@jax.custom_vjp
def low(v):
    return lax.optimization_barrier(v.astype(jnp.bfloat16)).astype(jnp.float32)

@jax.custom_vjp
def low_back(v):
    return v

def low_keep(v):
    return (low(v), None)

def low_pass(kept, grad):
    return (grad,)

def back_keep(v):
    return (v, None)

def back_low(kept, grad):
    return (low(grad),)
low.defvjp(low_keep, low_pass)
low_back.defvjp(back_keep, back_low)

def adamw_update(weight, moment, second, gradient, step_rate):
    moment = BETA_ONE * moment + (1.0 - BETA_ONE) * gradient
    second = BETA_TWO * second + (1.0 - BETA_TWO) * gradient * gradient
    moment_hat = moment / (1.0 - BETA_ONE ** ADAM_STEP)
    second_hat = second / (1.0 - BETA_TWO ** ADAM_STEP)
    weight = weight - step_rate * (moment_hat / (jnp.sqrt(second_hat) + ADAM_EPS) + DECAY * weight)
    return (weight, moment, second)

def reference(inputs, col_mask, row_mask, width_class, frequencies, phases, targets, prior_draws, hidden_weight, hidden_moment, hidden_second, alpha_weight, alpha_moment, alpha_second):
    onehot = (width_class[:, None] == jnp.arange(CLASSES, dtype=jnp.int32)[None, :]).astype(jnp.float32)
    keep_cols = jnp.dot(onehot, col_mask.astype(jnp.float32), precision=PRECISE)
    masked = inputs.astype(jnp.float32) * keep_cols
    keep_rows = row_mask.astype(jnp.float32)
    freq_full = frequencies.astype(jnp.float32)
    feat_scale = (2.0 / F) ** 0.5
    true_count = jnp.maximum(jnp.sum(keep_rows), 1.0)

    def forward(weight, alpha):
        first_pre = low_back(jnp.dot(masked, low(weight), precision=PRECISE))
        hidden = low(jnp.tanh(first_pre))
        pre = low_back(jnp.dot(hidden, freq_full, precision=PRECISE))
        features = low(feat_scale * jnp.cos(pre + phases[None, :]))
        alpha_low = low(alpha)
        moments = jnp.dot(features.T, alpha_low, precision=PRECISE)
        fitted = jnp.dot(features, moments, precision=PRECISE) + NOISE * alpha
        residual = low_back(fitted - targets[:, None] - prior_draws)
        squares = jnp.sum(keep_rows[:, None] * residual * residual)
        return (squares / (true_count * S), squares)
    loss_value, pull, squares = jax.vjp(forward, hidden_weight, alpha_weight, has_aux=True)
    weight_grad, alpha_grad = pull(jnp.ones((), jnp.float32))
    norm_before = jnp.sqrt(jnp.sum(weight_grad * weight_grad) + jnp.sum(alpha_grad * alpha_grad))
    resid_norm = jnp.sqrt(squares)
    clip = jnp.minimum(1.0, CLIP_AT / (norm_before + 1e-06))
    hidden_out, moment_out, second_out = adamw_update(hidden_weight, hidden_moment, hidden_second, weight_grad * clip, 0.02)
    alpha_out, alpha_moment_out, alpha_second_out = adamw_update(alpha_weight, alpha_moment, alpha_second, alpha_grad * clip, 0.05)
    return (norm_before, resid_norm, hidden_out, moment_out, second_out, hidden_out.astype(jnp.bfloat16), alpha_out, alpha_moment_out, alpha_second_out, alpha_out.astype(jnp.bfloat16))
```

```python
import jax
import jax.numpy as jnp
from jax import lax
from jax.sharding import PartitionSpec as P

ADAM_STEP = 10
NOISE = 0.01
CLIP_AT = 0.01
BETA_ONE = 0.9
BETA_TWO = 0.999
ADAM_EPS = 1e-08
DECAY = 0.01
CHUNKS = 2
LANES = 128
BF = jnp.bfloat16
F32 = jnp.float32


def adamw_update(weight, moment, second, gradient, step_rate):
    moment = BETA_ONE * moment + (1.0 - BETA_ONE) * gradient
    second = BETA_TWO * second + (1.0 - BETA_TWO) * gradient * gradient
    moment_hat = moment / (1.0 - BETA_ONE**ADAM_STEP)
    second_hat = second / (1.0 - BETA_TWO**ADAM_STEP)
    weight = weight - step_rate * (moment_hat / (jnp.sqrt(second_hat) + ADAM_EPS) + DECAY * weight)
    return (weight, moment, second)


def swap(x, axis, size, mask):
    return lax.ppermute(x, axis, [(i, i ^ mask) for i in range(size)])


def dot(a, b, dims):
    return lax.dot_general(a, b, (dims, ((), ())), preferred_element_type=F32)


def split_low(x):
    high = x.astype(BF)
    return high, (x - high.astype(F32)).astype(BF)


def reduce_angle(x):
    turns = jnp.round(x * 0.6366197723675814)
    rest = x - turns * 1.5703125
    rest = rest - turns * 0.00048351287841796875
    rest = rest - turns * 3.1385570764541626e-07
    rest = rest - turns * 6.077100628276711e-11
    return turns.astype(jnp.int32), rest


def sin_poly(r):
    s = r * r
    return r + r * s * (-1.6666654611e-1 + s * (8.3321608736e-3 + s * (-1.9515295891e-4)))


def cos_poly(r):
    s = r * r
    return 1.0 - 0.5 * s + s * s * (4.166664568298827e-2 + s * (-1.388731625493765e-3 + s * 2.443315711809948e-5))


def cosine(x):
    turns, rest = reduce_angle(x)
    value = jnp.where((turns & 1) == 0, cos_poly(rest), sin_poly(rest))
    return jnp.where(((turns + 1) & 2) == 0, value, -value)


def sine(x):
    turns, rest = reduce_angle(x)
    value = jnp.where((turns & 1) == 0, sin_poly(rest), cos_poly(rest))
    return jnp.where((turns & 2) == 0, value, -value)


def groups_of(size):
    bits = [1 << k for k in range(size.bit_length() - 1)]
    groups = [bits[:1]]
    if len(bits) > 2:
        groups.append([bits[1], bits[2], bits[1] | bits[2]])
    groups += [[b] for b in bits[3:]]
    if len(bits) == 2:
        groups.append([bits[1]])
    return [g for g in groups if g]


def sum_over_blk(x, size):
    for group in groups_of(size):
        x = x + sum(swap(x, "blk", size, m) for m in group)
    return x


def build(n_blk, n_feat):
    masks = [1 << k for k in range(n_blk.bit_length() - 1)]
    order = [0]
    for m in reversed(masks):
        order = order + [p ^ m for p in order]

    def on_device(
        inputs,
        col_mask,
        row_mask,
        width_class,
        frequencies,
        phases,
        targets,
        prior_draws,
        hidden_weight,
        hidden_moment,
        hidden_second,
        alpha_weight,
        alpha_moment,
        alpha_second,
    ):
        classes, d_in = col_mask.shape
        rows = d_in // n_blk
        n_low = frequencies.shape[1]
        feat_scale = (2.0 / (n_low * n_feat)) ** 0.5
        samples = alpha_weight.shape[1]
        h_own = hidden_weight.shape[1]
        width = h_own // CHUNKS
        me = lax.axis_index("blk")
        half = lax.axis_index("feat")

        low = hidden_weight.astype(BF)
        gathered = []
        for c in range(CHUNKS):
            held = low[:, c * width : (c + 1) * width]
            for m in reversed(masks):
                held = jnp.concatenate([held, swap(held, "blk", n_blk, m)], axis=0)
            gathered.append(held)

        onehot = (width_class[:, None] == jnp.arange(classes, dtype=jnp.int32)[None, :]).astype(F32)
        keep_cols = jnp.dot(onehot, col_mask.astype(F32))
        masked = inputs * keep_cols.astype(BF)
        column = jnp.arange(d_in, dtype=jnp.int32)
        source = (jnp.asarray(order, jnp.int32) ^ me)[column // rows] * rows + column % rows
        select = (column[:, None] == source[None, :]).astype(BF)
        masked = jnp.dot(masked, select, preferred_element_type=F32).astype(BF)
        keep_rows = row_mask.astype(F32)
        own_freq = lax.dynamic_slice_in_dim(frequencies, half * h_own, h_own, 0)
        far_freq = lax.dynamic_slice_in_dim(frequencies, (1 - half) * h_own, h_own, 0)

        tanhs = []
        pre = None
        for c in range(CHUNKS):
            first_pre = dot(masked, gathered[c], ((1,), (0,)))
            tanh_full = jnp.tanh(first_pre)
            hidden = tanh_full.astype(BF)
            far = swap(hidden, "feat", n_feat, 1)
            part = slice(c * width, (c + 1) * width)
            term = dot(hidden, own_freq[part], ((1,), (0,))) + dot(far, far_freq[part], ((1,), (0,)))
            pre = term if pre is None else pre + term
            tanhs.append(tanh_full)
        phase_arg = pre + phases[None, :]
        features = (feat_scale * cosine(phase_arg)).astype(BF)
        slope = -feat_scale * sine(phase_arg)

        alpha = alpha_weight.T
        alpha_low = alpha.astype(BF)
        count_here = jnp.sum(keep_rows)
        moments = dot(alpha_low, features, ((1,), (0,)))
        moments = jnp.concatenate([moments, jnp.full((samples, LANES), count_here, F32)], axis=1)
        moments = sum_over_blk(moments, n_blk)
        true_count = jnp.maximum(moments[0, n_low], 1.0)
        moments_hl = split_low(moments[:, :n_low])
        both = dot(jnp.concatenate(moments_hl, axis=0), features, ((1,), (1,)))
        fitted = both[:samples] + both[samples:]
        fitted = fitted + swap(fitted, "feat", n_feat, 1)
        residual = fitted + NOISE * alpha - targets[None, :] - prior_draws.T
        resid_grad = (2.0 * keep_rows[None, :] * residual / (true_count * samples)).astype(BF)
        squares_here = jnp.sum(keep_rows[None, :] * residual * residual)
        back = dot(resid_grad, features, ((1,), (0,)))
        back = jnp.concatenate([back, jnp.full((samples, LANES), squares_here, F32)], axis=1)
        back = sum_over_blk(back, n_blk)
        resid_norm = jnp.sqrt(back[0, n_low])
        back_hl = split_low(back[:, :n_low])

        left = jnp.concatenate([resid_grad, resid_grad, alpha_low, alpha_low], axis=0)
        right = jnp.concatenate([*moments_hl, *back_hl], axis=0)
        feature_grad = dot(left, right, ((0,), (0,)))
        pre_grad = (slope * feature_grad).astype(BF)

        both = dot(jnp.concatenate(back_hl, axis=0), features, ((1,), (1,)))
        pulled = both[:samples] + both[samples:]

        weight_grad = []
        arrived = []
        for c in range(CHUNKS):
            part = slice(c * width, (c + 1) * width)
            away = dot(pre_grad, far_freq[part], ((1,), (1,))).astype(BF)
            arrived.append(swap(away, "feat", n_feat, 1))
        pulled = pulled + swap(pulled, "feat", n_feat, 1)
        alpha_grad = pulled + NOISE * resid_grad.astype(F32)
        for c in range(CHUNKS):
            part = slice(c * width, (c + 1) * width)
            hidden_grad = dot(pre_grad, own_freq[part], ((1,), (1,))) + arrived[c].astype(F32)
            first_grad = ((1.0 - tanhs[c] * tanhs[c]) * hidden_grad).astype(BF)
            mid = d_in // 2
            send = dot(masked[:, mid:], first_grad, ((0,), (0,))).astype(BF)
            keep = dot(masked[:, :mid], first_grad, ((0,), (0,)))
            for m in masks:
                keep = keep + swap(send, "blk", n_blk, m).astype(F32)
                mid = mid // 2
                send = keep[mid:].astype(BF)
                keep = keep[:mid] if m != masks[-1] else keep
            weight_grad.append(keep)
        weight_grad = jnp.concatenate(weight_grad, axis=1)

        first_feat = (half == 0).astype(F32)
        grad_part = jnp.sum(weight_grad * weight_grad) + first_feat * jnp.sum(alpha_grad * alpha_grad)
        spread = jnp.broadcast_to(grad_part, (n_blk * n_feat, LANES))
        spread = lax.all_to_all(spread, ("blk", "feat"), 0, 0, tiled=True)
        norm_before = jnp.sqrt(jnp.sum(spread[:, 0]))
        clip = jnp.minimum(1.0, CLIP_AT / (norm_before + 1e-06))
        hidden_out, moment_out, second_out = adamw_update(
            hidden_weight, hidden_moment, hidden_second, weight_grad * clip, 0.02
        )
        alpha_out, alpha_moment_out, alpha_second_out = adamw_update(
            alpha_weight, alpha_moment, alpha_second, alpha_grad.T * clip, 0.05
        )
        return (
            norm_before,
            resid_norm,
            hidden_out,
            moment_out,
            second_out,
            hidden_out.astype(BF),
            alpha_out,
            alpha_moment_out,
            alpha_second_out,
            alpha_out.astype(BF),
        )

    return on_device


def solution(mesh):
    in_specs = (
        P("blk", None),
        P(),
        P("blk"),
        P("blk"),
        P(None, "feat"),
        P("feat"),
        P("blk"),
        P("blk", None),
        P("blk", "feat"),
        P("blk", "feat"),
        P("blk", "feat"),
        P("blk", None),
        P("blk", None),
        P("blk", None),
    )
    out_specs = (
        P(),
        P(),
        P("blk", "feat"),
        P("blk", "feat"),
        P("blk", "feat"),
        P("blk", "feat"),
        P("blk", None),
        P("blk", None),
        P("blk", None),
        P("blk", None),
    )
    on_device = build(mesh.shape["blk"], mesh.shape["feat"])
    return jax.shard_map(
        on_device, mesh=mesh, in_specs=in_specs, out_specs=out_specs, check_vma=False
    )
```

```python
import jax
import jax.numpy as jnp
from jax import lax
from jax.experimental import pallas as pl
from jax.experimental.pallas import tpu as pltpu
from jax.sharding import Mesh
from jax.sharding import PartitionSpec as P

ADAM_STEP = 10
NOISE = 0.01
CLIP_AT = 0.01
BETA_ONE = 0.9
BETA_TWO = 0.999
ADAM_EPS = 1e-08
DECAY = 0.01
CHUNKS = 2
LANES = 128
SCRATCH = 16 << 20
BIAS_A = 1
BIAS_C = 1
BF = jnp.bfloat16
F32 = jnp.float32
BLK = ("hi", "core")


def adamw_update(weight, moment, second, gradient, step_rate):
    moment = BETA_ONE * moment + (1.0 - BETA_ONE) * gradient
    second = BETA_TWO * second + (1.0 - BETA_TWO) * gradient * gradient
    moment_hat = moment / (1.0 - BETA_ONE**ADAM_STEP)
    second_hat = second / (1.0 - BETA_TWO**ADAM_STEP)
    weight = weight - step_rate * (moment_hat / (jnp.sqrt(second_hat) + ADAM_EPS) + DECAY * weight)
    return (weight, moment, second)


def swap(x, axis, size, mask):
    return lax.ppermute(x, axis, [(i, i ^ mask) for i in range(size)])


def dot(a, b, dims=((1,), (0,))):
    return lax.dot_general(a, b, (dims, ((), ())), preferred_element_type=F32)


def split_low(x):
    high = x.astype(BF)
    return high, (x - high.astype(F32)).astype(BF)


def sine_cosine(x):
    turns = jnp.round(x * 0.6366197723675814)
    rest = x - turns * 1.5703125
    rest = rest - turns * 0.00048351287841796875
    rest = rest - turns * 3.1385570764541626e-07
    rest = rest - turns * 6.077100628276711e-11
    turns = turns.astype(jnp.int32)
    s = rest * rest
    sin_part = rest + rest * s * (-1.6666654611e-1 + s * (8.3321608736e-3 + s * (-1.9515295891e-4)))
    cos_part = 1.0 - 0.5 * s + s * s * (
        4.166664568298827e-2 + s * (-1.388731625493765e-3 + s * 2.443315711809948e-5)
    )
    even = (turns & 1) == 0
    sine = jnp.where(even, sin_part, cos_part)
    cosine = jnp.where(even, cos_part, sin_part)
    sine = jnp.where((turns & 2) == 0, sine, -sine)
    cosine = jnp.where(((turns + 1) & 2) == 0, cosine, -cosine)
    return sine, cosine


def groups_of(size):
    bits = [1 << k for k in range(1, size.bit_length() - 1)]
    if len(bits) < 2:
        return [bits]
    return [[bits[0], bits[1], bits[0] | bits[1]]] + [[b] for b in bits[2:]]


def call(name, body, outs, *args, last=False, weight=1):
    shapes = jax.ShapeDtypeStruct if last else pltpu.VMEM
    return pl.pallas_call(
        body,
        out_shape=[shapes(shape, dtype) for shape, dtype in outs],
        cost_estimate=pl.CostEstimate(flops=weight, transcendentals=0, bytes_accessed=1),
        compiler_params=pltpu.CompilerParams(vmem_limit_bytes=SCRATCH),
        name=name,
    )(*[pltpu.with_memory_space_constraint(x, pltpu.VMEM) for x in args])


def my_half():
    return lax.axis_index("feat")


def turned(x):
    own = x.shape[0] // 2
    core = lax.axis_index("core")
    low, high = x[:own], x[own:]
    return jnp.concatenate(
        [jnp.where(core == 0, low, high), jnp.where(core == 0, high, low)], axis=0
    )


def freq_rows(freq_ref, half, start, count):
    total = freq_ref.shape[0] // 2
    return freq_ref[pl.ds(pl.multiple_of(half * total + start, count), count), :]


def prepare(inputs, width_class, col_mask, masked):
    d_in = inputs.shape[1]
    n_blk = lax.axis_size("hi") * 2
    rows = d_in // n_blk
    classes = col_mask.shape[0]
    me = lax.axis_index("hi") * 2 + lax.axis_index("core")
    chosen = width_class[...] == lax.broadcasted_iota(jnp.int32, (classes, inputs.shape[0]), 0)
    keep_cols = dot(chosen.astype(F32), col_mask[...].astype(F32), ((0,), (0,)))
    plain = inputs[...] * keep_cols.astype(BF)
    tile = min(256, d_in)
    n_bits, shift = n_blk.bit_length() - 1, rows.bit_length() - 1
    for t in range(d_in // tile):
        column = lax.broadcasted_iota(jnp.int32, (1, tile), 1) + t * tile
        place = column >> shift
        source = jnp.zeros_like(place)
        for k in range(n_bits):
            source = source | (((place >> k) & 1) << (n_bits - 1 - k))
        source = ((source ^ me) << shift) | (column & (rows - 1))
        select = lax.broadcasted_iota(jnp.int32, (d_in, tile), 0) == source
        select = jnp.where(select, 1.0, 0.0).astype(BF)
        masked[:, t * tile : (t + 1) * tile] = dot(plain, select).astype(BF)


def hidden_units(masked, held, hidden, damp):
    value = jnp.tanh(dot(masked[...], held[...]))
    hidden[...] = value.astype(BF)
    damp[...] = 1.0 - value * value


def own_pre(first, second, freq, phases, pre):
    width = first.shape[1]
    half = my_half()
    value = dot(first[...], freq_rows(freq, half, 0, width))
    value = value + dot(second[...], freq_rows(freq, half, width, width))
    pre[...] = value + phases[...]


def far_pre(pre, far, freq, out):
    out[...] = pre[...] + dot(far[...], freq_rows(freq, 1 - my_half(), 0, far.shape[1]))


def payload(keep, send, value, scalar):
    own = keep.shape[0]
    n_low = value.shape[1]
    keep[:, :n_low] = value[:own]
    keep[:, n_low:] = jnp.full((own, LANES), scalar, F32)
    send[:, :n_low] = value[own:]
    send[:, n_low:] = jnp.full((own, LANES), scalar, F32)


def make_features(pre, far, freq, alpha, row_mask, features, slope, keep, send):
    width = far.shape[1]
    scale = (2.0 / (pre.shape[1] * lax.axis_size("feat"))) ** 0.5
    angle = pre[...] + dot(far[...], freq_rows(freq, 1 - my_half(), width, width))
    sine, cosine = sine_cosine(angle)
    value = (scale * cosine).astype(BF)
    features[...] = value
    slope[...] = -scale * sine
    moments = dot(turned(alpha[...]).astype(BF), value)
    payload(keep, send, moments, jnp.sum(row_mask[...].astype(F32)))


def fit(mine, other, features, moments, fitted):
    n_low = features.shape[1]
    value = jnp.concatenate([mine[:, :n_low], other[:, :n_low]], axis=0)
    parts = jnp.concatenate(split_low(value), axis=0)
    moments[...] = parts
    both = dot(parts, features[...], ((1,), (1,)))
    samples = value.shape[0]
    fitted[...] = both[:samples] + both[samples:]


def residuals(near, far, mine, alpha, targets, prior, row_mask, features, resid_grad, keep, send):
    samples = alpha.shape[0]
    n_low = features.shape[1]
    true_count = jnp.maximum(mine[0:1, n_low : n_low + 1], 1.0)
    residual = near[...] + far[...] + NOISE * turned(alpha[...]) - targets[...] - turned(prior[...])
    keep_rows = row_mask[...].astype(F32)
    value = (2.0 * keep_rows * residual / (true_count * samples)).astype(BF)
    resid_grad[...] = value
    payload(keep, send, dot(value, features[...]), jnp.sum(keep_rows * residual * residual))


def pre_gradient(mine, other, moments, resid_grad, alpha, slope, freq, back, pre_grad, away):
    n_low = slope.shape[1]
    value = jnp.concatenate([mine[:, :n_low], other[:, :n_low]], axis=0)
    parts = jnp.concatenate(split_low(value), axis=0)
    back[...] = parts
    low = turned(alpha[...]).astype(BF)
    resid = resid_grad[...]
    left = jnp.concatenate([resid, resid, low, low], axis=0)
    right = jnp.concatenate([moments[...], parts], axis=0)
    grad = (slope[...] * dot(left, right, ((0,), (0,)))).astype(BF)
    pre_grad[...] = grad
    away[...] = dot(grad, freq_rows(freq, 1 - my_half(), 0, away.shape[1]), ((1,), (1,))).astype(BF)


def second_away(pre_grad, freq, away):
    width = away.shape[1]
    away[...] = dot(
        pre_grad[...], freq_rows(freq, 1 - my_half(), width, width), ((1,), (1,))
    ).astype(BF)


def own_gradient(pre_grad, freq, back, features, near, pulled):
    near[...] = dot(pre_grad[...], freq_rows(freq, my_half(), 0, near.shape[1]), ((1,), (1,)))
    both = dot(back[...], features[...], ((1,), (1,)))
    samples = pulled.shape[0]
    pulled[...] = both[:samples] + both[samples:]


def weight_terms(part):
    def body(near, got, damp, masked, *refs):
        *pulls, send, keep = refs if len(refs) == 2 else refs[:-1]
        hidden_grad = near[:, part] + got[...].astype(F32)
        first_grad = (damp[...] * hidden_grad).astype(BF)
        mid = send.shape[0]
        send[...] = dot(masked[:, mid:], first_grad, ((0,), (0,))).astype(BF)
        keep[...] = dot(masked[:, :mid], first_grad, ((0,), (0,)))
        if pulls:
            pulled, pulled_far, resid_grad = pulls
            refs[-1][...] = pulled[...] + pulled_far[...] + NOISE * resid_grad[...].astype(F32)

    return body


def add_halves(keep, got, send, rest):
    mid = rest.shape[0]
    send[...] = (keep[mid:] + got[mid:].astype(F32)).astype(BF)
    rest[...] = keep[:mid] + got[:mid].astype(F32)


def finish_gradients(keep, got, *refs):
    *earlier, weight_grad, total = refs
    value = keep[...] + got[...].astype(F32)
    weight_grad[...] = value
    whole = jnp.sum(value * value)
    if earlier:
        alpha_grad, before = earlier
        own = alpha_grad[...]
        whole = whole + before[0, 0] + jnp.where(my_half() == 0, jnp.sum(own * own), 0.0)
    total[...] = jnp.full(total.shape, whole, F32)


def update(*refs):
    spread, squares, *grads = refs[: 2 + CHUNKS]
    alpha_grad, *refs = refs[2 + CHUNKS :]
    weight, moment, second, alpha, alpha_moment, alpha_second = refs[:6]
    norm_out, resid_out = refs[6:8]
    norm = jnp.sqrt(jnp.sum(spread[:, :, 0:1], axis=0))
    norm_out[...] = norm
    last = squares.shape[1] - 1
    resid_out[...] = jnp.sqrt(squares[0:1, last:])
    clip = jnp.minimum(1.0, CLIP_AT / (norm + 1e-06))
    width = weight.shape[1] // CHUNKS
    work = [
        (slice(c * width, (c + 1) * width), (weight, moment, second), grad[...], 0.02, refs[8:12])
        for c, grad in enumerate(grads)
    ]
    held = (alpha, alpha_moment, alpha_second)
    work.append((slice(None), held, turned(alpha_grad[...]), 0.05, refs[12:16]))
    for part, values, grad, rate, outs in work:
        new = adamw_update(*[v[:, part] for v in values], grad * clip, rate)
        for out, value in zip(outs, (*new, new[0].astype(BF))):
            out[:, part] = value


def build(n_blk, n_feat):
    masks = [1 << k for k in range(n_blk.bit_length() - 1)]
    size = n_blk * n_feat

    def sum_over_blk(keep, send):
        keep = keep + swap(send, BLK, n_blk, 1)
        for group in groups_of(n_blk):
            keep = keep + sum(swap(keep, BLK, n_blk, m) for m in group)
        return keep, swap(keep, BLK, n_blk, 1)

    def on_device(
        inputs,
        col_mask,
        row_mask,
        width_class,
        frequencies,
        phases,
        targets,
        prior_draws,
        hidden_weight,
        hidden_moment,
        hidden_second,
        alpha_weight,
        alpha_moment,
        alpha_second,
    ):
        d_in = col_mask.shape[1]
        points, samples = alpha_weight.shape
        n_low = frequencies.shape[1]
        h_own = hidden_weight.shape[1]
        width = h_own // CHUNKS
        row_mask, width_class, phases, targets = (
            x.reshape(1, -1) for x in (row_mask, width_class, phases, targets)
        )
        alpha, prior = alpha_weight.T, prior_draws.T

        low = hidden_weight.astype(BF)
        (masked,) = call(
            "prepare", prepare, [((points, d_in), BF)], inputs, width_class, col_mask
        )
        units = [((points, width), BF), ((points, width), F32)]
        hidden, damps = [], []
        for c in range(CHUNKS):
            held = low[:, c * width : (c + 1) * width]
            for m in reversed(masks):
                held = jnp.concatenate([held, swap(held, BLK, n_blk, m)], axis=0)
            unit, damp = call("hidden", hidden_units, units, masked, held)
            hidden.append(unit)
            damps.append(damp)
        fars = [swap(h, "feat", n_feat, 1) for h in hidden]
        wide = ((points, n_low), F32)
        (pre,) = call("own_pre", own_pre, [wide], *hidden, frequencies, phases)
        (pre,) = call("far_pre", far_pre, [wide], pre, fars[0], frequencies, weight=BIAS_A)
        pair = [((samples // 2, n_low + LANES), F32)] * 2
        features, slope, keep, send = call(
            "features",
            make_features,
            [((points, n_low), BF), wide, *pair],
            pre,
            fars[1],
            frequencies,
            alpha,
            row_mask,
        )
        mine, other = sum_over_blk(keep, send)
        parts = ((2 * samples, n_low), BF)
        thin = ((samples, points), F32)
        moments, fitted = call("fit", fit, [parts, thin], mine, other, features)
        fitted_far = swap(fitted, "feat", n_feat, 1)
        resid_grad, keep, send = call(
            "residuals",
            residuals,
            [((samples, points), BF), *pair],
            fitted,
            fitted_far,
            mine,
            alpha,
            targets,
            prior,
            row_mask,
            features,
        )
        mine, other = sum_over_blk(keep, send)
        away = ((points, width), BF)
        back, pre_grad, first = call(
            "pre_gradient",
            pre_gradient,
            [parts, ((points, n_low), BF), away],
            mine,
            other,
            moments,
            resid_grad,
            alpha,
            slope,
            frequencies,
        )
        gots = [swap(first, "feat", n_feat, 1)]
        (second,) = call("second_away", second_away, [away], pre_grad, frequencies)
        gots.append(swap(second, "feat", n_feat, 1))
        near, pulled = call(
            "own_gradient",
            own_gradient,
            [((points, h_own), F32), thin],
            pre_grad,
            frequencies,
            back,
            features,
        )
        pulled_far = swap(pulled, "feat", n_feat, 1)

        grads, totals = [], []
        for c in range(CHUNKS):
            mid = d_in // 2
            shapes = [((mid, width), BF), ((mid, width), F32)]
            part = slice(c * width, (c + 1) * width)
            operands = [near, gots[c], damps[c], masked]
            if c == CHUNKS - 1:
                operands += [pulled, pulled_far, resid_grad]
                shapes = shapes + [thin]
            send, keep, *alpha_grad = call("weight_terms", weight_terms(part), shapes, *operands)
            for m in masks[:-1]:
                got = swap(send, BLK, n_blk, m)
                mid = mid // 2
                shapes = [((mid, width), BF), ((mid, width), F32)]
                send, keep = call("add_halves", add_halves, shapes, keep, got)
            got = swap(send, BLK, n_blk, masks[-1])
            last = c == CHUNKS - 1
            outs = [((mid, width), F32), ((size, 1, LANES) if last else (1, LANES), F32)]
            grad, total = call(
                "finish",
                finish_gradients,
                outs,
                keep,
                got,
                *alpha_grad,
                *totals,
                weight=1 if last else BIAS_C,
            )
            grads.append(grad)
            totals = [total]
        (spread,) = totals
        spread = lax.all_to_all(spread, (*BLK, "feat"), 0, 0, tiled=True)
        scalar = ((1, 1), F32)
        big, small = hidden_weight.shape, (samples, points)
        outs = call(
            "update",
            update,
            [scalar, scalar]
            + [(big, F32)] * 3
            + [(big, BF)]
            + [(small, F32)] * 3
            + [(small, BF)],
            spread,
            mine,
            *grads,
            *alpha_grad,
            hidden_weight,
            hidden_moment,
            hidden_second,
            alpha,
            alpha_moment.T,
            alpha_second.T,
            last=True,
        )
        norm, resid = outs[:2]
        return (norm[0, 0], resid[0, 0], *outs[2:6], *[x.T for x in outs[6:]])

    return on_device


def solution(mesh):
    in_specs = (
        P(BLK, None),
        P(),
        P(BLK),
        P(BLK),
        P(None, "feat"),
        P("feat"),
        P(BLK),
        P(BLK, None),
        P(BLK, "feat"),
        P(BLK, "feat"),
        P(BLK, "feat"),
        P(BLK, None),
        P(BLK, None),
        P(BLK, None),
    )
    out_specs = (
        P(),
        P(),
        P(BLK, "feat"),
        P(BLK, "feat"),
        P(BLK, "feat"),
        P(BLK, "feat"),
        P(BLK, None),
        P(BLK, None),
        P(BLK, None),
        P(BLK, None),
    )
    n_blk, n_feat = mesh.shape["blk"], mesh.shape["feat"]
    inner = Mesh(mesh.devices.reshape(n_blk // 2, 2, n_feat), (*BLK, "feat"))
    on_device = build(n_blk, n_feat)
    return jax.shard_map(
        on_device, mesh=inner, in_specs=in_specs, out_specs=out_specs, check_vma=False
    )
```

```python
import jax
import jax.numpy as jnp
from jax import lax
from jax.experimental import pallas as pl
from jax.experimental.pallas import tpu as pltpu
from jax.sharding import Mesh
from jax.sharding import PartitionSpec as P

ADAM_STEP = 10
NOISE = 0.01
CLIP_AT = 0.01
BETA_ONE = 0.9
BETA_TWO = 0.999
ADAM_EPS = 1e-08
DECAY = 0.01
SHARES = (3, 5)
CHUNKS = len(SHARES)
TOGETHER = 1
LANES = 128
SCRATCH = 16 << 20
BIAS_A = 8_000_000_000
BIAS_C = 1
T1 = 1
T2 = 0
BF = jnp.bfloat16
F32 = jnp.float32
BLK = ("hi", "core")


def adamw_update(weight, moment, second, gradient, step_rate):
    moment = BETA_ONE * moment + (1.0 - BETA_ONE) * gradient
    second = BETA_TWO * second + (1.0 - BETA_TWO) * gradient * gradient
    moment_hat = moment / (1.0 - BETA_ONE**ADAM_STEP)
    second_hat = second / (1.0 - BETA_TWO**ADAM_STEP)
    weight = weight - step_rate * (moment_hat / (jnp.sqrt(second_hat) + ADAM_EPS) + DECAY * weight)
    return (weight, moment, second)


def swap(x, axis, size, mask):
    return lax.ppermute(x, axis, [(i, i ^ mask) for i in range(size)])


def dot(a, b, dims=((1,), (0,))):
    return lax.dot_general(a, b, (dims, ((), ())), preferred_element_type=F32)


def after(x, earlier):
    return lax.optimization_barrier((x, earlier))[0]


def split_low(x):
    high = x.astype(BF)
    return high, (x - high.astype(F32)).astype(BF)


def sine_cosine(x):
    turns = jnp.round(x * 0.6366197723675814)
    rest = x - turns * 1.5703125
    rest = rest - turns * 0.00048351287841796875
    rest = rest - turns * 3.1385570764541626e-07
    rest = rest - turns * 6.077100628276711e-11
    turns = turns.astype(jnp.int32)
    s = rest * rest
    sin_part = rest + rest * s * (-1.6666654611e-1 + s * (8.3321608736e-3 + s * (-1.9515295891e-4)))
    cos_part = 1.0 - 0.5 * s + s * s * (
        4.166664568298827e-2 + s * (-1.388731625493765e-3 + s * 2.443315711809948e-5)
    )
    even = (turns & 1) == 0
    sine = jnp.where(even, sin_part, cos_part)
    cosine = jnp.where(even, cos_part, sin_part)
    sine = jnp.where((turns & 2) == 0, sine, -sine)
    cosine = jnp.where(((turns + 1) & 2) == 0, cosine, -cosine)
    return sine, cosine


def groups_of(size):
    bits = [1 << k for k in range(1, size.bit_length() - 1)]
    if len(bits) < 2:
        return [bits]
    return [[bits[0], bits[1], bits[0] | bits[1]]] + [[b] for b in bits[2:]]


def call(name, body, outs, *args, last=False, weight=1):
    shapes = jax.ShapeDtypeStruct if last else pltpu.VMEM
    return pl.pallas_call(
        body,
        out_shape=[shapes(shape, dtype) for shape, dtype in outs],
        cost_estimate=pl.CostEstimate(flops=weight, transcendentals=0, bytes_accessed=1),
        compiler_params=pltpu.CompilerParams(vmem_limit_bytes=SCRATCH),
        name=name,
    )(*[pltpu.with_memory_space_constraint(x, pltpu.VMEM) for x in args])


def my_half():
    return lax.axis_index("feat")


def turned(x):
    own = x.shape[0] // 2
    core = lax.axis_index("core")
    low, high = x[:own], x[own:]
    return jnp.concatenate(
        [jnp.where(core == 0, low, high), jnp.where(core == 0, high, low)], axis=0
    )


def freq_rows(freq_ref, half, start, count):
    total = freq_ref.shape[0] // 2
    return freq_ref[pl.ds(pl.multiple_of(half * total + start, LANES), count), :]


def pieces_of(whole):
    ends = [whole * sum(SHARES[:k]) // sum(SHARES) for k in range(CHUNKS + 1)]
    return [slice(a, b) for a, b in zip(ends[:-1], ends[1:])]


def core_halves(mid):
    core = lax.axis_index("core")
    return [pl.ds(pl.multiple_of(k * mid, LANES), mid) for k in (core, 1 - core)]


def prepare(inputs, width_class, col_mask, masked):
    d_in = inputs.shape[1]
    n_blk = lax.axis_size("hi") * 2
    rows = d_in // n_blk
    classes = col_mask.shape[0]
    me = lax.axis_index("hi") * 2
    chosen = width_class[...] == lax.broadcasted_iota(jnp.int32, (classes, inputs.shape[0]), 0)
    keep_cols = dot(chosen.astype(F32), col_mask[...].astype(F32), ((0,), (0,)))
    plain = inputs[...] * keep_cols.astype(BF)
    tile = min(256, d_in)
    n_bits, shift = n_blk.bit_length() - 1, rows.bit_length() - 1
    for t in range(d_in // tile):
        column = lax.broadcasted_iota(jnp.int32, (1, tile), 1) + t * tile
        place = column >> shift
        source = jnp.zeros_like(place)
        for k in range(n_bits):
            source = source | (((place >> k) & 1) << (n_bits - 1 - k))
        source = ((source ^ me) << shift) | (column & (rows - 1))
        select = lax.broadcasted_iota(jnp.int32, (d_in, tile), 0) == source
        select = jnp.where(select, 1.0, 0.0).astype(BF)
        masked[:, t * tile : (t + 1) * tile] = dot(plain, select).astype(BF)


def hidden_units(masked, *refs):
    helds, (hidden, damp) = refs[: 1 if len(refs) == 3 else 2], refs[-2:]
    if len(helds) == 1:
        value = dot(masked[...], helds[0][...])
    else:
        parts = core_halves(masked.shape[1] // 2)
        value = sum(dot(masked[:, part], held[...]) for part, held in zip(parts, helds))
    value = jnp.tanh(value)
    hidden[...] = value.astype(BF)
    damp[...] = 1.0 - value * value


def first_pre(hidden, far, freq, phases, pre):
    width = hidden.shape[1]
    value = phases[...] + dot(hidden[...], freq_rows(freq, my_half(), 0, width))
    pre[...] = value + dot(far[...], freq_rows(freq, 1 - my_half(), 0, width))


def second_pre(pre, hidden, freq, out):
    width = hidden.shape[1]
    start = freq.shape[0] // 2 - width
    out[...] = pre[...] + dot(hidden[...], freq_rows(freq, my_half(), start, width))


def payload(keep, send, value, scalar):
    own = keep.shape[0]
    n_low = value.shape[1]
    keep[:, :n_low] = value[:own]
    keep[:, n_low:] = jnp.full((own, LANES), scalar, F32)
    send[:, :n_low] = value[own:]
    send[:, n_low:] = jnp.full((own, LANES), scalar, F32)


def make_features(pre, far, freq, alpha, row_mask, features, slope, keep, send):
    width = far.shape[1]
    scale = (2.0 / (pre.shape[1] * lax.axis_size("feat"))) ** 0.5
    start = freq.shape[0] // 2 - width
    angle = pre[...] + dot(far[...], freq_rows(freq, 1 - my_half(), start, width))
    sine, cosine = sine_cosine(angle)
    value = (scale * cosine).astype(BF)
    features[...] = value
    slope[...] = -scale * sine
    moments = dot(turned(alpha[...]).astype(BF), value)
    payload(keep, send, moments, jnp.sum(row_mask[...].astype(F32)))


def fit(mine, other, features, moments, fitted):
    n_low = features.shape[1]
    value = jnp.concatenate([mine[:, :n_low], other[:, :n_low]], axis=0)
    parts = jnp.concatenate(split_low(value), axis=0)
    moments[...] = parts
    both = dot(parts, features[...], ((1,), (1,)))
    samples = value.shape[0]
    fitted[...] = both[:samples] + both[samples:]


def residuals(near, far, mine, alpha, targets, prior, row_mask, features, resid_grad, keep, send):
    samples = alpha.shape[0]
    n_low = features.shape[1]
    true_count = jnp.maximum(mine[0:1, n_low : n_low + 1], 1.0)
    residual = near[...] + far[...] + NOISE * turned(alpha[...]) - targets[...] - turned(prior[...])
    keep_rows = row_mask[...].astype(F32)
    value = (2.0 * keep_rows * residual / (true_count * samples)).astype(BF)
    resid_grad[...] = value
    payload(keep, send, dot(value, features[...]), jnp.sum(keep_rows * residual * residual))


def pre_gradient(mine, other, moments, resid_grad, alpha, slope, freq, back, pre_grad, away):
    n_low = slope.shape[1]
    value = jnp.concatenate([mine[:, :n_low], other[:, :n_low]], axis=0)
    parts = jnp.concatenate(split_low(value), axis=0)
    back[...] = parts
    low = turned(alpha[...]).astype(BF)
    resid = resid_grad[...]
    left = jnp.concatenate([resid, resid, low, low], axis=0)
    right = jnp.concatenate([moments[...], parts], axis=0)
    grad = (slope[...] * dot(left, right, ((0,), (0,)))).astype(BF)
    pre_grad[...] = grad
    away[...] = dot(grad, freq_rows(freq, 1 - my_half(), 0, away.shape[1]), ((1,), (1,))).astype(BF)


def second_away(pre_grad, freq, away):
    width = away.shape[1]
    start = freq.shape[0] // 2 - width
    away[...] = dot(
        pre_grad[...], freq_rows(freq, 1 - my_half(), start, width), ((1,), (1,))
    ).astype(BF)


def own_gradient(pre_grad, freq, back, features, near, pulled):
    near[...] = dot(pre_grad[...], freq_rows(freq, my_half(), 0, near.shape[1]), ((1,), (1,)))
    both = dot(back[...], features[...], ((1,), (1,)))
    samples = pulled.shape[0]
    pulled[...] = both[:samples] + both[samples:]


def weight_terms(part):
    def body(near, got, damp, masked, *refs):
        *pulls, send, keep = refs if len(refs) == 2 else refs[:-1]
        hidden_grad = near[:, part] + got[...].astype(F32)
        first_grad = (damp[...] * hidden_grad).astype(BF)
        mid = send.shape[0]
        own, other = core_halves(mid)
        send[...] = dot(masked[:, other], first_grad, ((0,), (0,))).astype(BF)
        keep[...] = dot(masked[:, own], first_grad, ((0,), (0,)))
        if pulls:
            pulled, pulled_far, resid_grad = pulls
            refs[-1][...] = pulled[...] + pulled_far[...] + NOISE * resid_grad[...].astype(F32)

    return body


def add_halves(keep, got, send, rest):
    mid = rest.shape[0]
    start = 0
    if got.shape[0] != keep.shape[0]:
        start = pl.multiple_of((1 - lax.axis_index("core")) * 2 * mid, mid)
    send[...] = (keep[mid:] + got[pl.ds(start + mid, mid)].astype(F32)).astype(BF)
    rest[...] = keep[:mid] + got[pl.ds(start, mid)].astype(F32)


def finish_gradients(keep, got, *refs):
    *earlier, weight_grad, total = refs
    value = keep[...] + got[...].astype(F32)
    weight_grad[...] = value
    whole = jnp.sum(value * value)
    if earlier:
        alpha_grad, before = earlier
        own = alpha_grad[...]
        whole = whole + before[0, 0] + jnp.where(my_half() == 0, jnp.sum(own * own), 0.0)
    total[...] = jnp.full(total.shape, whole, F32)


def update(*refs):
    spread, squares, *grads = refs[: 2 + CHUNKS]
    alpha_grad, *refs = refs[2 + CHUNKS :]
    weight, moment, second, alpha, alpha_moment, alpha_second = refs[:6]
    norm_out, resid_out = refs[6:8]
    norm = jnp.sqrt(jnp.sum(spread[:, :, 0:1], axis=0))
    norm_out[...] = norm
    last = squares.shape[1] - 1
    resid_out[...] = jnp.sqrt(squares[0:1, last:])
    clip = jnp.minimum(1.0, CLIP_AT / (norm + 1e-06))
    work = [
        (part, (weight, moment, second), grad[...], 0.02, refs[8:12])
        for part, grad in zip(pieces_of(weight.shape[1]), grads)
    ]
    held = (alpha, alpha_moment, alpha_second)
    work.append((slice(None), held, turned(alpha_grad[...]), 0.05, refs[12:16]))
    for part, values, grad, rate, outs in work:
        new = adamw_update(*[v[:, part] for v in values], grad * clip, rate)
        for out, value in zip(outs, (*new, new[0].astype(BF))):
            out[:, part] = value


def build(n_blk, n_feat):
    masks = [1 << k for k in range(n_blk.bit_length() - 1)]
    size = n_blk * n_feat

    def sum_over_blk(keep, send):
        keep = keep + swap(send, BLK, n_blk, 1)
        for group in groups_of(n_blk):
            keep = keep + sum(swap(keep, BLK, n_blk, m) for m in group)
        return keep, swap(keep, BLK, n_blk, 1)

    def on_device(
        inputs,
        col_mask,
        row_mask,
        width_class,
        frequencies,
        phases,
        targets,
        prior_draws,
        hidden_weight,
        hidden_moment,
        hidden_second,
        alpha_weight,
        alpha_moment,
        alpha_second,
    ):
        d_in = col_mask.shape[1]
        points, samples = alpha_weight.shape
        n_low = frequencies.shape[1]
        h_own = hidden_weight.shape[1]
        pieces = pieces_of(h_own)
        widths = [p.stop - p.start for p in pieces]
        row_mask, width_class, phases, targets = (
            x.reshape(1, -1) for x in (row_mask, width_class, phases, targets)
        )
        alpha, prior = alpha_weight.T, prior_draws.T

        low = hidden_weight.astype(BF)
        (masked,) = call(
            "prepare", prepare, [((points, d_in), BF)], inputs, width_class, col_mask
        )
        partly = []
        for c in range(CHUNKS):
            held = low[:, pieces[c]]
            for k, m in enumerate(reversed(masks[1:])):
                held = jnp.concatenate([held, swap(held, BLK, n_blk, m)], axis=0)
                if c == 0 and k == 0:
                    held = after(held, masked)
            partly.append(held)
        units = [[((points, w), BF), ((points, w), F32)] for w in widths]
        wide = ((points, n_low), F32)
        held = lax.all_gather(partly[0], "core", axis=0, tiled=True)
        hidden, damp = call("hidden", hidden_units, units[0], masked, held)
        partly[1] = after(partly[1], hidden)
        far = swap(hidden, "feat", n_feat, 1)
        (pre,) = call(
            "first_pre", first_pre, [wide], hidden, far, frequencies, phases, weight=BIAS_A
        )
        helds = [partly[1], swap(partly[1], BLK, n_blk, 1)]
        hidden, damp_b = call("hidden", hidden_units, units[1], masked, *helds, pre)
        damps = [damp, damp_b]
        far = swap(hidden, "feat", n_feat, 1)
        (pre,) = call("second_pre", second_pre, [wide], pre, hidden, frequencies)
        pair = [((samples // 2, n_low + LANES), F32)] * 2
        features, slope, keep, send = call(
            "features",
            make_features,
            [((points, n_low), BF), wide, *pair],
            pre,
            far,
            frequencies,
            alpha,
            row_mask,
        )
        mine, other = sum_over_blk(keep, send)
        parts = ((2 * samples, n_low), BF)
        thin = ((samples, points), F32)
        moments, fitted = call("fit", fit, [parts, thin], mine, other, features)
        fitted_far = swap(fitted, "feat", n_feat, 1)
        resid_grad, keep, send = call(
            "residuals",
            residuals,
            [((samples, points), BF), *pair],
            fitted,
            fitted_far,
            mine,
            alpha,
            targets,
            prior,
            row_mask,
            features,
        )
        mine, other = sum_over_blk(keep, send)
        away = [((points, width), BF) for width in widths]
        back, pre_grad, first = call(
            "pre_gradient",
            pre_gradient,
            [parts, ((points, n_low), BF), away[0]],
            mine,
            other,
            moments,
            resid_grad,
            alpha,
            slope,
            frequencies,
        )
        gots = [swap(first, "feat", n_feat, 1)]
        (second,) = call("second_away", second_away, away[1:], pre_grad, frequencies)
        gots.append(swap(second, "feat", n_feat, 1))
        near, pulled = call(
            "own_gradient",
            own_gradient,
            [((points, h_own), F32), thin],
            pre_grad,
            frequencies,
            back,
            features,
        )
        pulled_far = swap(pulled, "feat", n_feat, 1)

        grads, totals = [], []
        for c in range(CHUNKS):
            mid = d_in // 2
            width = widths[c]
            shapes = [((mid, width), BF), ((mid, width), F32)]
            operands = [near, gots[c], damps[c], masked]
            if T2 and c:
                operands[2] = after(damps[c], early)
            if c == CHUNKS - 1:
                operands += [pulled, pulled_far, resid_grad]
                shapes = shapes + [thin]
            send, keep, *alpha_grad = call("weight_terms", weight_terms(pieces[c]), shapes, *operands)
            for m in masks[:-1]:
                if c < TOGETHER and m == masks[0]:
                    got = lax.all_gather(send, "core", axis=0, tiled=True)
                else:
                    got = swap(send, BLK, n_blk, m)
                mid = mid // 2
                shapes = [((mid, width), BF), ((mid, width), F32)]
                ahead = c == 0 and m == masks[1]
                if T1 and c and m == masks[0]:
                    keep = after(keep, sent)
                weight = BIAS_C if ahead else 1
                send, keep = call("add_halves", add_halves, shapes, keep, got, weight=weight)
                if ahead:
                    sent = send
                if c == 0 and m == masks[0]:
                    early = send
            got = swap(send, BLK, n_blk, masks[-1])
            last = c == CHUNKS - 1
            outs = [((mid, width), F32), ((size, 1, LANES) if last else (1, LANES), F32)]
            grad, total = call(
                "finish",
                finish_gradients,
                outs,
                keep,
                got,
                *alpha_grad,
                *totals,
            )
            grads.append(grad)
            totals = [total]
        (spread,) = totals
        spread = lax.all_to_all(spread, (*BLK, "feat"), 0, 0, tiled=True)
        scalar = ((1, 1), F32)
        big, small = hidden_weight.shape, (samples, points)
        outs = call(
            "update",
            update,
            [scalar, scalar]
            + [(big, F32)] * 3
            + [(big, BF)]
            + [(small, F32)] * 3
            + [(small, BF)],
            spread,
            mine,
            *grads,
            *alpha_grad,
            hidden_weight,
            hidden_moment,
            hidden_second,
            alpha,
            alpha_moment.T,
            alpha_second.T,
            last=True,
        )
        norm, resid = outs[:2]
        return (norm[0, 0], resid[0, 0], *outs[2:6], *[x.T for x in outs[6:]])

    return on_device


def solution(mesh):
    in_specs = (
        P(BLK, None),
        P(),
        P(BLK),
        P(BLK),
        P(None, "feat"),
        P("feat"),
        P(BLK),
        P(BLK, None),
        P(BLK, "feat"),
        P(BLK, "feat"),
        P(BLK, "feat"),
        P(BLK, None),
        P(BLK, None),
        P(BLK, None),
    )
    out_specs = (
        P(),
        P(),
        P(BLK, "feat"),
        P(BLK, "feat"),
        P(BLK, "feat"),
        P(BLK, "feat"),
        P(BLK, None),
        P(BLK, None),
        P(BLK, None),
        P(BLK, None),
    )
    n_blk, n_feat = mesh.shape["blk"], mesh.shape["feat"]
    inner = Mesh(mesh.devices.reshape(n_blk // 2, 2, n_feat), (*BLK, "feat"))
    on_device = build(n_blk, n_feat)
    return jax.shard_map(
        on_device, mesh=inner, in_specs=in_specs, out_specs=out_specs, check_vma=False
    )
```

```python
import jax
import jax.numpy as jnp
from jax import lax
from jax.experimental import pallas as pl
from jax.experimental.pallas import tpu as pltpu
from jax.sharding import Mesh
from jax.sharding import PartitionSpec as P

ADAM_STEP = 10
NOISE = 0.01
CLIP_AT = 0.01
BETA_ONE = 0.9
BETA_TWO = 0.999
ADAM_EPS = 1e-08
DECAY = 0.01
SHARES = (3, 5)
CHUNKS = len(SHARES)
TOGETHER = 1
LANES = 128
SCRATCH = 16 << 20
BIAS_A = 8_000_000_000
BIAS_C = 1
T1 = 0
T2 = 0
BF = jnp.bfloat16
F32 = jnp.float32
BLK = ("hi", "core")


def adamw_update(weight, moment, second, gradient, step_rate):
    moment = BETA_ONE * moment + (1.0 - BETA_ONE) * gradient
    second = BETA_TWO * second + (1.0 - BETA_TWO) * gradient * gradient
    moment_hat = moment / (1.0 - BETA_ONE**ADAM_STEP)
    second_hat = second / (1.0 - BETA_TWO**ADAM_STEP)
    weight = weight - step_rate * (moment_hat / (jnp.sqrt(second_hat) + ADAM_EPS) + DECAY * weight)
    return (weight, moment, second)


def swap(x, axis, size, mask):
    return lax.ppermute(x, axis, [(i, i ^ mask) for i in range(size)])


def dot(a, b, dims=((1,), (0,))):
    return lax.dot_general(a, b, (dims, ((), ())), preferred_element_type=F32)


def after(x, earlier):
    return lax.optimization_barrier((x, earlier))[0]


def split_low(x):
    high = x.astype(BF)
    return high, (x - high.astype(F32)).astype(BF)


def sine_cosine(x):
    turns = jnp.round(x * 0.6366197723675814)
    rest = x - turns * 1.5703125
    rest = rest - turns * 0.00048351287841796875
    rest = rest - turns * 3.1385570764541626e-07
    rest = rest - turns * 6.077100628276711e-11
    turns = turns.astype(jnp.int32)
    s = rest * rest
    sin_part = rest + rest * s * (-1.6666654611e-1 + s * (8.3321608736e-3 + s * (-1.9515295891e-4)))
    cos_part = 1.0 - 0.5 * s + s * s * (
        4.166664568298827e-2 + s * (-1.388731625493765e-3 + s * 2.443315711809948e-5)
    )
    even = (turns & 1) == 0
    sine = jnp.where(even, sin_part, cos_part)
    cosine = jnp.where(even, cos_part, sin_part)
    sine = jnp.where((turns & 2) == 0, sine, -sine)
    cosine = jnp.where(((turns + 1) & 2) == 0, cosine, -cosine)
    return sine, cosine


def groups_of(size):
    bits = [1 << k for k in range(1, size.bit_length() - 1)]
    if len(bits) < 2:
        return [bits]
    return [[bits[0], bits[1], bits[0] | bits[1]]] + [[b] for b in bits[2:]]


def call(name, body, outs, *args, last=False, weight=1):
    shapes = jax.ShapeDtypeStruct if last else pltpu.VMEM
    return pl.pallas_call(
        body,
        out_shape=[shapes(shape, dtype) for shape, dtype in outs],
        cost_estimate=pl.CostEstimate(flops=weight, transcendentals=0, bytes_accessed=1),
        compiler_params=pltpu.CompilerParams(vmem_limit_bytes=SCRATCH),
        name=name,
    )(*[pltpu.with_memory_space_constraint(x, pltpu.VMEM) for x in args])


def my_half():
    return lax.axis_index("feat")


def turned(x):
    own = x.shape[0] // 2
    core = lax.axis_index("core")
    low, high = x[:own], x[own:]
    return jnp.concatenate(
        [jnp.where(core == 0, low, high), jnp.where(core == 0, high, low)], axis=0
    )


def freq_rows(freq_ref, half, start, count):
    total = freq_ref.shape[0] // 2
    return freq_ref[pl.ds(pl.multiple_of(half * total + start, LANES), count), :]


def pieces_of(whole):
    ends = [whole * sum(SHARES[:k]) // sum(SHARES) for k in range(CHUNKS + 1)]
    return [slice(a, b) for a, b in zip(ends[:-1], ends[1:])]


def core_halves(mid):
    core = lax.axis_index("core")
    return [pl.ds(pl.multiple_of(k * mid, LANES), mid) for k in (core, 1 - core)]


def prepare(inputs, width_class, col_mask, masked):
    d_in = inputs.shape[1]
    n_blk = lax.axis_size("hi") * 2
    rows = d_in // n_blk
    classes = col_mask.shape[0]
    me = lax.axis_index("hi") * 2
    chosen = width_class[...] == lax.broadcasted_iota(jnp.int32, (classes, inputs.shape[0]), 0)
    keep_cols = dot(chosen.astype(F32), col_mask[...].astype(F32), ((0,), (0,)))
    plain = inputs[...] * keep_cols.astype(BF)
    tile = min(256, d_in)
    n_bits, shift = n_blk.bit_length() - 1, rows.bit_length() - 1
    for t in range(d_in // tile):
        column = lax.broadcasted_iota(jnp.int32, (1, tile), 1) + t * tile
        place = column >> shift
        source = jnp.zeros_like(place)
        for k in range(n_bits):
            source = source | (((place >> k) & 1) << (n_bits - 1 - k))
        source = ((source ^ me) << shift) | (column & (rows - 1))
        select = lax.broadcasted_iota(jnp.int32, (d_in, tile), 0) == source
        select = jnp.where(select, 1.0, 0.0).astype(BF)
        masked[:, t * tile : (t + 1) * tile] = dot(plain, select).astype(BF)


def hidden_units(masked, *refs):
    helds, (hidden, damp) = refs[: 1 if len(refs) == 3 else 2], refs[-2:]
    if len(helds) == 1:
        value = dot(masked[...], helds[0][...])
    else:
        parts = core_halves(masked.shape[1] // 2)
        value = sum(dot(masked[:, part], held[...]) for part, held in zip(parts, helds))
    value = jnp.tanh(value)
    hidden[...] = value.astype(BF)
    damp[...] = 1.0 - value * value


def first_pre(hidden, far, freq, phases, pre):
    width = hidden.shape[1]
    value = phases[...] + dot(hidden[...], freq_rows(freq, my_half(), 0, width))
    pre[...] = value + dot(far[...], freq_rows(freq, 1 - my_half(), 0, width))


def second_pre(pre, hidden, freq, out):
    width = hidden.shape[1]
    start = freq.shape[0] // 2 - width
    out[...] = pre[...] + dot(hidden[...], freq_rows(freq, my_half(), start, width))


def payload(keep, send, value, scalar):
    own = keep.shape[0]
    n_low = value.shape[1]
    keep[:, :n_low] = value[:own]
    keep[:, n_low:] = jnp.full((own, LANES), scalar, F32)
    send[:, :n_low] = value[own:]
    send[:, n_low:] = jnp.full((own, LANES), scalar, F32)


def make_features(pre, far, freq, alpha, row_mask, features, slope, keep, send):
    width = far.shape[1]
    scale = (2.0 / (pre.shape[1] * lax.axis_size("feat"))) ** 0.5
    start = freq.shape[0] // 2 - width
    angle = pre[...] + dot(far[...], freq_rows(freq, 1 - my_half(), start, width))
    sine, cosine = sine_cosine(angle)
    value = (scale * cosine).astype(BF)
    features[...] = value
    slope[...] = -scale * sine
    moments = dot(turned(alpha[...]).astype(BF), value)
    payload(keep, send, moments, jnp.sum(row_mask[...].astype(F32)))


def fit(mine, other, features, moments, fitted):
    n_low = features.shape[1]
    value = jnp.concatenate([mine[:, :n_low], other[:, :n_low]], axis=0)
    parts = jnp.concatenate(split_low(value), axis=0)
    moments[...] = parts
    both = dot(parts, features[...], ((1,), (1,)))
    samples = value.shape[0]
    fitted[...] = both[:samples] + both[samples:]


def residuals(near, far, mine, alpha, targets, prior, row_mask, features, resid_grad, keep, send):
    samples = alpha.shape[0]
    n_low = features.shape[1]
    true_count = jnp.maximum(mine[0:1, n_low : n_low + 1], 1.0)
    residual = near[...] + far[...] + NOISE * turned(alpha[...]) - targets[...] - turned(prior[...])
    keep_rows = row_mask[...].astype(F32)
    value = (2.0 * keep_rows * residual / (true_count * samples)).astype(BF)
    resid_grad[...] = value
    payload(keep, send, dot(value, features[...]), jnp.sum(keep_rows * residual * residual))


def pre_gradient(mine, other, moments, resid_grad, alpha, slope, freq, back, pre_grad, away):
    n_low = slope.shape[1]
    value = jnp.concatenate([mine[:, :n_low], other[:, :n_low]], axis=0)
    parts = jnp.concatenate(split_low(value), axis=0)
    back[...] = parts
    low = turned(alpha[...]).astype(BF)
    resid = resid_grad[...]
    left = jnp.concatenate([resid, resid, low, low], axis=0)
    right = jnp.concatenate([moments[...], parts], axis=0)
    grad = (slope[...] * dot(left, right, ((0,), (0,)))).astype(BF)
    pre_grad[...] = grad
    away[...] = dot(grad, freq_rows(freq, 1 - my_half(), 0, away.shape[1]), ((1,), (1,))).astype(BF)


def second_away(pre_grad, freq, away):
    width = away.shape[1]
    start = freq.shape[0] // 2 - width
    away[...] = dot(
        pre_grad[...], freq_rows(freq, 1 - my_half(), start, width), ((1,), (1,))
    ).astype(BF)


def own_gradient(pre_grad, freq, back, features, near, pulled):
    near[...] = dot(pre_grad[...], freq_rows(freq, my_half(), 0, near.shape[1]), ((1,), (1,)))
    both = dot(back[...], features[...], ((1,), (1,)))
    samples = pulled.shape[0]
    pulled[...] = both[:samples] + both[samples:]


def weight_terms(part):
    def body(near, got, damp, masked, *refs):
        *pulls, send, keep = refs if len(refs) == 2 else refs[:-1]
        hidden_grad = near[:, part] + got[...].astype(F32)
        first_grad = (damp[...] * hidden_grad).astype(BF)
        mid = send.shape[0]
        own, other = core_halves(mid)
        send[...] = dot(masked[:, other], first_grad, ((0,), (0,))).astype(BF)
        keep[...] = dot(masked[:, own], first_grad, ((0,), (0,)))
        if pulls:
            pulled, pulled_far, resid_grad = pulls
            refs[-1][...] = pulled[...] + pulled_far[...] + NOISE * resid_grad[...].astype(F32)

    return body


def add_halves(keep, got, send, rest):
    mid = rest.shape[0]
    start = 0
    if got.shape[0] != keep.shape[0]:
        start = pl.multiple_of((1 - lax.axis_index("core")) * 2 * mid, mid)
    send[...] = (keep[mid:] + got[pl.ds(start + mid, mid)].astype(F32)).astype(BF)
    rest[...] = keep[:mid] + got[pl.ds(start, mid)].astype(F32)


def finish_gradients(keep, got, *refs):
    *earlier, weight_grad, total = refs
    value = keep[...] + got[...].astype(F32)
    weight_grad[...] = value
    whole = jnp.sum(value * value)
    if earlier:
        alpha_grad, before = earlier
        own = alpha_grad[...]
        whole = whole + before[0, 0] + jnp.where(my_half() == 0, jnp.sum(own * own), 0.0)
    total[...] = jnp.full(total.shape, whole, F32)


def update(*refs):
    spread, squares, *grads = refs[: 2 + CHUNKS]
    alpha_grad, *refs = refs[2 + CHUNKS :]
    weight, moment, second, alpha, alpha_moment, alpha_second = refs[:6]
    norm_out, resid_out = refs[6:8]
    norm = jnp.sqrt(jnp.sum(spread[:, :, 0:1], axis=0))
    norm_out[...] = norm
    last = squares.shape[1] - 1
    resid_out[...] = jnp.sqrt(squares[0:1, last:])
    clip = jnp.minimum(1.0, CLIP_AT / (norm + 1e-06))
    work = [
        (part, (weight, moment, second), grad[...], 0.02, refs[8:12])
        for part, grad in zip(pieces_of(weight.shape[1]), grads)
    ]
    held = (alpha, alpha_moment, alpha_second)
    work.append((slice(None), held, turned(alpha_grad[...]), 0.05, refs[12:16]))
    for part, values, grad, rate, outs in work:
        new = adamw_update(*[v[:, part] for v in values], grad * clip, rate)
        for out, value in zip(outs, (*new, new[0].astype(BF))):
            out[:, part] = value


def build(n_blk, n_feat):
    masks = [1 << k for k in range(n_blk.bit_length() - 1)]
    size = n_blk * n_feat

    def sum_over_blk(keep, send):
        keep = keep + swap(send, BLK, n_blk, 1)
        for group in groups_of(n_blk):
            keep = keep + sum(swap(keep, BLK, n_blk, m) for m in group)
        return keep, swap(keep, BLK, n_blk, 1)

    def on_device(
        inputs,
        col_mask,
        row_mask,
        width_class,
        frequencies,
        phases,
        targets,
        prior_draws,
        hidden_weight,
        hidden_moment,
        hidden_second,
        alpha_weight,
        alpha_moment,
        alpha_second,
    ):
        d_in = col_mask.shape[1]
        points, samples = alpha_weight.shape
        n_low = frequencies.shape[1]
        h_own = hidden_weight.shape[1]
        pieces = pieces_of(h_own)
        widths = [p.stop - p.start for p in pieces]
        row_mask, width_class, phases, targets = (
            x.reshape(1, -1) for x in (row_mask, width_class, phases, targets)
        )
        alpha, prior = alpha_weight.T, prior_draws.T

        low = hidden_weight.astype(BF)
        (masked,) = call(
            "prepare", prepare, [((points, d_in), BF)], inputs, width_class, col_mask
        )
        partly = []
        for c in range(CHUNKS):
            held = low[:, pieces[c]]
            for k, m in enumerate(reversed(masks[1:])):
                held = jnp.concatenate([held, swap(held, BLK, n_blk, m)], axis=0)
                if c == 0 and k == 0:
                    held = after(held, masked)
            partly.append(held)
        units = [[((points, w), BF), ((points, w), F32)] for w in widths]
        wide = ((points, n_low), F32)
        held = lax.all_gather(partly[0], "core", axis=0, tiled=True)
        hidden, damp = call("hidden", hidden_units, units[0], masked, held)
        partly[1] = after(partly[1], hidden)
        far = swap(hidden, "feat", n_feat, 1)
        (pre,) = call(
            "first_pre", first_pre, [wide], hidden, far, frequencies, phases, weight=BIAS_A
        )
        helds = [partly[1], swap(partly[1], BLK, n_blk, 1)]
        hidden, damp_b = call("hidden", hidden_units, units[1], masked, *helds, pre)
        damps = [damp, damp_b]
        far = swap(hidden, "feat", n_feat, 1)
        (pre,) = call("second_pre", second_pre, [wide], pre, hidden, frequencies)
        pair = [((samples // 2, n_low + LANES), F32)] * 2
        features, slope, keep, send = call(
            "features",
            make_features,
            [((points, n_low), BF), wide, *pair],
            pre,
            far,
            frequencies,
            alpha,
            row_mask,
        )
        mine, other = sum_over_blk(keep, send)
        parts = ((2 * samples, n_low), BF)
        thin = ((samples, points), F32)
        moments, fitted = call("fit", fit, [parts, thin], mine, other, features)
        fitted_far = swap(fitted, "feat", n_feat, 1)
        resid_grad, keep, send = call(
            "residuals",
            residuals,
            [((samples, points), BF), *pair],
            fitted,
            fitted_far,
            mine,
            alpha,
            targets,
            prior,
            row_mask,
            features,
        )
        mine, other = sum_over_blk(keep, send)
        away = [((points, width), BF) for width in widths]
        back, pre_grad, first = call(
            "pre_gradient",
            pre_gradient,
            [parts, ((points, n_low), BF), away[0]],
            mine,
            other,
            moments,
            resid_grad,
            alpha,
            slope,
            frequencies,
        )
        gots = [swap(first, "feat", n_feat, 1)]
        (second,) = call("second_away", second_away, away[1:], pre_grad, frequencies)
        gots.append(swap(second, "feat", n_feat, 1))
        near, pulled = call(
            "own_gradient",
            own_gradient,
            [((points, h_own), F32), thin],
            pre_grad,
            frequencies,
            back,
            features,
        )
        pulled_far = swap(pulled, "feat", n_feat, 1)

        grads, totals = [], []
        for c in range(CHUNKS):
            mid = d_in // 2
            width = widths[c]
            shapes = [((mid, width), BF), ((mid, width), F32)]
            operands = [near, gots[c], damps[c], masked]
            if T2 and c:
                operands[2] = after(damps[c], early)
            if c == CHUNKS - 1:
                operands += [pulled, pulled_far, resid_grad]
                shapes = shapes + [thin]
            send, keep, *alpha_grad = call("weight_terms", weight_terms(pieces[c]), shapes, *operands)
            for m in masks[:-1]:
                if c < TOGETHER and m == masks[0]:
                    got = lax.all_gather(send, "core", axis=0, tiled=True)
                else:
                    got = swap(send, BLK, n_blk, m)
                mid = mid // 2
                shapes = [((mid, width), BF), ((mid, width), F32)]
                ahead = c == 0 and m == masks[1]
                if T1 and c and m == masks[0]:
                    keep = after(keep, sent)
                weight = BIAS_C if ahead else 1
                send, keep = call("add_halves", add_halves, shapes, keep, got, weight=weight)
                if ahead:
                    sent = send
                if c == 0 and m == masks[0]:
                    early = send
            got = swap(send, BLK, n_blk, masks[-1])
            last = c == CHUNKS - 1
            outs = [((mid, width), F32), ((size, 1, LANES) if last else (1, LANES), F32)]
            grad, total = call(
                "finish",
                finish_gradients,
                outs,
                keep,
                got,
                *alpha_grad,
                *totals,
            )
            grads.append(grad)
            totals = [total]
        (spread,) = totals
        spread = lax.all_to_all(spread, (*BLK, "feat"), 0, 0, tiled=True)
        scalar = ((1, 1), F32)
        big, small = hidden_weight.shape, (samples, points)
        outs = call(
            "update",
            update,
            [scalar, scalar]
            + [(big, F32)] * 3
            + [(big, BF)]
            + [(small, F32)] * 3
            + [(small, BF)],
            spread,
            mine,
            *grads,
            *alpha_grad,
            hidden_weight,
            hidden_moment,
            hidden_second,
            alpha,
            alpha_moment.T,
            alpha_second.T,
            last=True,
        )
        norm, resid = outs[:2]
        return (norm[0, 0], resid[0, 0], *outs[2:6], *[x.T for x in outs[6:]])

    return on_device


def solution(mesh):
    in_specs = (
        P(BLK, None),
        P(),
        P(BLK),
        P(BLK),
        P(None, "feat"),
        P("feat"),
        P(BLK),
        P(BLK, None),
        P(BLK, "feat"),
        P(BLK, "feat"),
        P(BLK, "feat"),
        P(BLK, None),
        P(BLK, None),
        P(BLK, None),
    )
    out_specs = (
        P(),
        P(),
        P(BLK, "feat"),
        P(BLK, "feat"),
        P(BLK, "feat"),
        P(BLK, "feat"),
        P(BLK, None),
        P(BLK, None),
        P(BLK, None),
        P(BLK, None),
    )
    n_blk, n_feat = mesh.shape["blk"], mesh.shape["feat"]
    inner = Mesh(mesh.devices.reshape(n_blk // 2, 2, n_feat), (*BLK, "feat"))
    on_device = build(n_blk, n_feat)
    return jax.shard_map(
        on_device, mesh=inner, in_specs=in_specs, out_specs=out_specs, check_vma=False
    )
```

```python
import jax
import jax.numpy as jnp
from jax import lax
from jax.experimental import pallas as pl
from jax.experimental.pallas import tpu as pltpu
from jax.sharding import Mesh
from jax.sharding import PartitionSpec as P

ADAM_STEP = 10
NOISE = 0.01
CLIP_AT = 0.01
BETA_ONE = 0.9
BETA_TWO = 0.999
ADAM_EPS = 1e-08
DECAY = 0.01
SHARES = (3, 5)
CHUNKS = len(SHARES)
TOGETHER = 1
LANES = 128
SCRATCH = 16 << 20
BIAS_A = 8_000_000_000
BF = jnp.bfloat16
F32 = jnp.float32
BLK = ("hi", "core")


def adamw_update(weight, moment, second, gradient, step_rate):
    moment = BETA_ONE * moment + (1.0 - BETA_ONE) * gradient
    second = BETA_TWO * second + (1.0 - BETA_TWO) * gradient * gradient
    moment_hat = moment / (1.0 - BETA_ONE**ADAM_STEP)
    second_hat = second / (1.0 - BETA_TWO**ADAM_STEP)
    weight = weight - step_rate * (moment_hat / (jnp.sqrt(second_hat) + ADAM_EPS) + DECAY * weight)
    return (weight, moment, second)


def swap(x, axis, size, mask):
    return lax.ppermute(x, axis, [(i, i ^ mask) for i in range(size)])


def dot(a, b, dims=((1,), (0,))):
    return lax.dot_general(a, b, (dims, ((), ())), preferred_element_type=F32)


def after(x, earlier):
    return lax.optimization_barrier((x, earlier))[0]


def split_low(x):
    high = x.astype(BF)
    return high, (x - high.astype(F32)).astype(BF)


def sine_cosine(x):
    turns = jnp.round(x * 0.6366197723675814)
    rest = x - turns * 1.5703125
    rest = rest - turns * 0.00048351287841796875
    rest = rest - turns * 3.1385570764541626e-07
    rest = rest - turns * 6.077100628276711e-11
    turns = turns.astype(jnp.int32)
    s = rest * rest
    sin_part = rest + rest * s * (-1.6666654611e-1 + s * (8.3321608736e-3 + s * (-1.9515295891e-4)))
    cos_part = 1.0 - 0.5 * s + s * s * (
        4.166664568298827e-2 + s * (-1.388731625493765e-3 + s * 2.443315711809948e-5)
    )
    even = (turns & 1) == 0
    sine = jnp.where(even, sin_part, cos_part)
    cosine = jnp.where(even, cos_part, sin_part)
    sine = jnp.where((turns & 2) == 0, sine, -sine)
    cosine = jnp.where(((turns + 1) & 2) == 0, cosine, -cosine)
    return sine, cosine


def groups_of(size):
    bits = [1 << k for k in range(1, size.bit_length() - 1)]
    if len(bits) < 2:
        return [bits]
    return [[bits[0], bits[1], bits[0] | bits[1]]] + [[b] for b in bits[2:]]


def call(name, body, outs, *args, last=False, weight=1):
    shapes = jax.ShapeDtypeStruct if last else pltpu.VMEM
    return pl.pallas_call(
        body,
        out_shape=[shapes(shape, dtype) for shape, dtype in outs],
        cost_estimate=pl.CostEstimate(flops=weight, transcendentals=0, bytes_accessed=1),
        compiler_params=pltpu.CompilerParams(vmem_limit_bytes=SCRATCH),
        name=name,
    )(*[pltpu.with_memory_space_constraint(x, pltpu.VMEM) for x in args])


def my_half():
    return lax.axis_index("feat")


def turned(x):
    own = x.shape[0] // 2
    core = lax.axis_index("core")
    low, high = x[:own], x[own:]
    return jnp.concatenate(
        [jnp.where(core == 0, low, high), jnp.where(core == 0, high, low)], axis=0
    )


def freq_rows(freq_ref, half, start, count):
    total = freq_ref.shape[0] // 2
    return freq_ref[pl.ds(pl.multiple_of(half * total + start, LANES), count), :]


def pieces_of(whole):
    ends = [whole * sum(SHARES[:k]) // sum(SHARES) for k in range(CHUNKS + 1)]
    return [slice(a, b) for a, b in zip(ends[:-1], ends[1:])]


def core_halves(mid):
    core = lax.axis_index("core")
    return [pl.ds(pl.multiple_of(k * mid, LANES), mid) for k in (core, 1 - core)]


def prepare(inputs, width_class, col_mask, masked):
    d_in = inputs.shape[1]
    n_blk = lax.axis_size("hi") * 2
    rows = d_in // n_blk
    classes = col_mask.shape[0]
    me = lax.axis_index("hi") * 2
    chosen = width_class[...] == lax.broadcasted_iota(jnp.int32, (classes, inputs.shape[0]), 0)
    keep_cols = dot(chosen.astype(F32), col_mask[...].astype(F32), ((0,), (0,)))
    plain = inputs[...] * keep_cols.astype(BF)
    tile = min(256, d_in)
    n_bits, shift = n_blk.bit_length() - 1, rows.bit_length() - 1
    for t in range(d_in // tile):
        column = lax.broadcasted_iota(jnp.int32, (1, tile), 1) + t * tile
        place = column >> shift
        source = jnp.zeros_like(place)
        for k in range(n_bits):
            source = source | (((place >> k) & 1) << (n_bits - 1 - k))
        source = ((source ^ me) << shift) | (column & (rows - 1))
        select = lax.broadcasted_iota(jnp.int32, (d_in, tile), 0) == source
        select = jnp.where(select, 1.0, 0.0).astype(BF)
        masked[:, t * tile : (t + 1) * tile] = dot(plain, select).astype(BF)


def hidden_units(masked, *refs):
    helds, (hidden, damp) = refs[: 1 if len(refs) == 3 else 2], refs[-2:]
    if len(helds) == 1:
        value = dot(masked[...], helds[0][...])
    else:
        parts = core_halves(masked.shape[1] // 2)
        value = sum(dot(masked[:, part], held[...]) for part, held in zip(parts, helds))
    value = jnp.tanh(value)
    hidden[...] = value.astype(BF)
    damp[...] = 1.0 - value * value


def first_pre(hidden, far, freq, phases, pre):
    width = hidden.shape[1]
    value = phases[...] + dot(hidden[...], freq_rows(freq, my_half(), 0, width))
    pre[...] = value + dot(far[...], freq_rows(freq, 1 - my_half(), 0, width))


def second_pre(pre, hidden, freq, out):
    width = hidden.shape[1]
    start = freq.shape[0] // 2 - width
    out[...] = pre[...] + dot(hidden[...], freq_rows(freq, my_half(), start, width))


def payload(keep, send, value, scalar):
    own = keep.shape[0]
    n_low = value.shape[1]
    keep[:, :n_low] = value[:own]
    keep[:, n_low:] = jnp.full((own, LANES), scalar, F32)
    send[:, :n_low] = value[own:]
    send[:, n_low:] = jnp.full((own, LANES), scalar, F32)


def make_features(pre, far, freq, alpha, row_mask, features, slope, keep, send):
    width = far.shape[1]
    scale = (2.0 / (pre.shape[1] * lax.axis_size("feat"))) ** 0.5
    start = freq.shape[0] // 2 - width
    angle = pre[...] + dot(far[...], freq_rows(freq, 1 - my_half(), start, width))
    sine, cosine = sine_cosine(angle)
    value = (scale * cosine).astype(BF)
    features[...] = value
    slope[...] = -scale * sine
    moments = dot(turned(alpha[...]).astype(BF), value)
    payload(keep, send, moments, jnp.sum(row_mask[...].astype(F32)))


def fit(mine, other, features, moments, fitted):
    n_low = features.shape[1]
    value = jnp.concatenate([mine[:, :n_low], other[:, :n_low]], axis=0)
    parts = jnp.concatenate(split_low(value), axis=0)
    moments[...] = parts
    both = dot(parts, features[...], ((1,), (1,)))
    samples = value.shape[0]
    fitted[...] = both[:samples] + both[samples:]


def residuals(near, far, mine, alpha, targets, prior, row_mask, features, resid_grad, keep, send):
    samples = alpha.shape[0]
    n_low = features.shape[1]
    true_count = jnp.maximum(mine[0:1, n_low : n_low + 1], 1.0)
    residual = near[...] + far[...] + NOISE * turned(alpha[...]) - targets[...] - turned(prior[...])
    keep_rows = row_mask[...].astype(F32)
    value = (2.0 * keep_rows * residual / (true_count * samples)).astype(BF)
    resid_grad[...] = value
    payload(keep, send, dot(value, features[...]), jnp.sum(keep_rows * residual * residual))


def pre_gradient(mine, other, moments, resid_grad, alpha, slope, freq, back, pre_grad, away):
    n_low = slope.shape[1]
    value = jnp.concatenate([mine[:, :n_low], other[:, :n_low]], axis=0)
    parts = jnp.concatenate(split_low(value), axis=0)
    back[...] = parts
    low = turned(alpha[...]).astype(BF)
    resid = resid_grad[...]
    left = jnp.concatenate([resid, resid, low, low], axis=0)
    right = jnp.concatenate([moments[...], parts], axis=0)
    grad = (slope[...] * dot(left, right, ((0,), (0,)))).astype(BF)
    pre_grad[...] = grad
    width = away.shape[1]
    start = freq.shape[0] // 2 - width
    away[...] = dot(grad, freq_rows(freq, 1 - my_half(), start, width), ((1,), (1,))).astype(BF)


def second_away(pre_grad, freq, away):
    width = away.shape[1]
    away[...] = dot(
        pre_grad[...], freq_rows(freq, 1 - my_half(), 0, width), ((1,), (1,))
    ).astype(BF)


def own_gradient(pre_grad, freq, back, features, near, pulled):
    near[...] = dot(pre_grad[...], freq_rows(freq, my_half(), 0, near.shape[1]), ((1,), (1,)))
    both = dot(back[...], features[...], ((1,), (1,)))
    samples = pulled.shape[0]
    pulled[...] = both[:samples] + both[samples:]


def weight_terms(part):
    def body(near, got, damp, masked, *refs):
        *pulls, send, keep = refs if len(refs) == 2 else refs[:-1]
        hidden_grad = near[:, part] + got[...].astype(F32)
        first_grad = (damp[...] * hidden_grad).astype(BF)
        mid = send.shape[0]
        own, other = core_halves(mid)
        send[...] = dot(masked[:, other], first_grad, ((0,), (0,))).astype(BF)
        keep[...] = dot(masked[:, own], first_grad, ((0,), (0,)))
        if pulls:
            pulled, pulled_far, resid_grad = pulls
            refs[-1][...] = pulled[...] + pulled_far[...] + NOISE * resid_grad[...].astype(F32)

    return body


def add_halves(keep, got, send, rest):
    mid = rest.shape[0]
    start = 0
    if got.shape[0] != keep.shape[0]:
        start = pl.multiple_of((1 - lax.axis_index("core")) * 2 * mid, mid)
    send[...] = (keep[mid:] + got[pl.ds(start + mid, mid)].astype(F32)).astype(BF)
    rest[...] = keep[:mid] + got[pl.ds(start, mid)].astype(F32)


def finish_gradients(keep, got, *refs):
    *earlier, weight_grad, total = refs
    value = keep[...] + got[...].astype(F32)
    weight_grad[...] = value
    whole = jnp.sum(value * value)
    if earlier:
        alpha_grad, before = earlier
        own = alpha_grad[...]
        whole = whole + before[0, 0] + jnp.where(my_half() == 0, jnp.sum(own * own), 0.0)
    total[...] = jnp.full(total.shape, whole, F32)


def update(*refs):
    spread, squares, *grads = refs[: 2 + CHUNKS]
    alpha_grad, *refs = refs[2 + CHUNKS :]
    weight, moment, second, alpha, alpha_moment, alpha_second = refs[:6]
    norm_out, resid_out = refs[6:8]
    norm = jnp.sqrt(jnp.sum(spread[:, :, 0:1], axis=0))
    norm_out[...] = norm
    last = squares.shape[1] - 1
    resid_out[...] = jnp.sqrt(squares[0:1, last:])
    clip = jnp.minimum(1.0, CLIP_AT / (norm + 1e-06))
    work = [
        (part, (weight, moment, second), grad[...], 0.02, refs[8:12])
        for part, grad in zip(pieces_of(weight.shape[1]), grads)
    ]
    held = (alpha, alpha_moment, alpha_second)
    work.append((slice(None), held, turned(alpha_grad[...]), 0.05, refs[12:16]))
    for part, values, grad, rate, outs in work:
        new = adamw_update(*[v[:, part] for v in values], grad * clip, rate)
        for out, value in zip(outs, (*new, new[0].astype(BF))):
            out[:, part] = value


def build(n_blk, n_feat):
    masks = [1 << k for k in range(n_blk.bit_length() - 1)]
    size = n_blk * n_feat

    def sum_over_blk(keep, send):
        keep = keep + swap(send, BLK, n_blk, 1)
        for group in groups_of(n_blk):
            keep = keep + sum(swap(keep, BLK, n_blk, m) for m in group)
        return keep, swap(keep, BLK, n_blk, 1)

    def on_device(
        inputs,
        col_mask,
        row_mask,
        width_class,
        frequencies,
        phases,
        targets,
        prior_draws,
        hidden_weight,
        hidden_moment,
        hidden_second,
        alpha_weight,
        alpha_moment,
        alpha_second,
    ):
        d_in = col_mask.shape[1]
        points, samples = alpha_weight.shape
        n_low = frequencies.shape[1]
        h_own = hidden_weight.shape[1]
        pieces = pieces_of(h_own)
        widths = [p.stop - p.start for p in pieces]
        row_mask, width_class, phases, targets = (
            x.reshape(1, -1) for x in (row_mask, width_class, phases, targets)
        )
        alpha, prior = alpha_weight.T, prior_draws.T

        low = hidden_weight.astype(BF)
        (masked,) = call(
            "prepare", prepare, [((points, d_in), BF)], inputs, width_class, col_mask
        )
        partly = []
        for c in range(CHUNKS):
            held = low[:, pieces[c]]
            for m in reversed(masks[1:]):
                held = jnp.concatenate([held, swap(held, BLK, n_blk, m)], axis=0)
            partly.append(held)
        units = [[((points, w), BF), ((points, w), F32)] for w in widths]
        wide = ((points, n_low), F32)
        held = lax.all_gather(partly[0], "core", axis=0, tiled=True)
        hidden, damp = call("hidden", hidden_units, units[0], masked, held)
        partly[1] = after(partly[1], hidden)
        far = swap(hidden, "feat", n_feat, 1)
        (pre,) = call(
            "first_pre", first_pre, [wide], hidden, far, frequencies, phases, weight=BIAS_A
        )
        helds = [partly[1], swap(partly[1], BLK, n_blk, 1)]
        hidden, damp_b = call("hidden", hidden_units, units[1], masked, *helds, pre)
        damps = [damp, damp_b]
        far = swap(hidden, "feat", n_feat, 1)
        (pre,) = call("second_pre", second_pre, [wide], pre, hidden, frequencies)
        pair = [((samples // 2, n_low + LANES), F32)] * 2
        features, slope, keep, send = call(
            "features",
            make_features,
            [((points, n_low), BF), wide, *pair],
            pre,
            far,
            frequencies,
            alpha,
            row_mask,
        )
        mine, other = sum_over_blk(keep, send)
        parts = ((2 * samples, n_low), BF)
        thin = ((samples, points), F32)
        moments, fitted = call("fit", fit, [parts, thin], mine, other, features)
        fitted_far = swap(fitted, "feat", n_feat, 1)
        resid_grad, keep, send = call(
            "residuals",
            residuals,
            [((samples, points), BF), *pair],
            fitted,
            fitted_far,
            mine,
            alpha,
            targets,
            prior,
            row_mask,
            features,
        )
        mine, other = sum_over_blk(keep, send)
        away = [((points, width), BF) for width in widths]
        back, pre_grad, first = call(
            "pre_gradient",
            pre_gradient,
            [parts, ((points, n_low), BF), away[1]],
            mine,
            other,
            moments,
            resid_grad,
            alpha,
            slope,
            frequencies,
        )
        gots = [swap(first, "feat", n_feat, 1)]
        (second,) = call("second_away", second_away, away[:1], pre_grad, frequencies)
        gots.insert(0, swap(second, "feat", n_feat, 1))
        near, pulled = call(
            "own_gradient",
            own_gradient,
            [((points, h_own), F32), thin],
            pre_grad,
            frequencies,
            back,
            features,
        )
        pulled_far = swap(pulled, "feat", n_feat, 1)

        grads, totals = [], []
        for c in reversed(range(CHUNKS)):
            mid = d_in // 2
            width = widths[c]
            shapes = [((mid, width), BF), ((mid, width), F32)]
            operands = [near, gots[c], damps[c], masked]
            if c == 0:
                operands += [pulled, pulled_far, resid_grad]
                shapes = shapes + [thin]
            send, keep, *alpha_grad = call("weight_terms", weight_terms(pieces[c]), shapes, *operands)
            for m in masks[:-1]:
                if c < TOGETHER and m == masks[0]:
                    got = lax.all_gather(send, "core", axis=0, tiled=True)
                else:
                    got = swap(send, BLK, n_blk, m)
                mid = mid // 2
                shapes = [((mid, width), BF), ((mid, width), F32)]
                send, keep = call("add_halves", add_halves, shapes, keep, got)
            got = swap(send, BLK, n_blk, masks[-1])
            last = c == 0
            outs = [((mid, width), F32), ((size, 1, LANES) if last else (1, LANES), F32)]
            grad, total = call(
                "finish",
                finish_gradients,
                outs,
                keep,
                got,
                *alpha_grad,
                *totals,
            )
            grads.insert(0, grad)
            totals = [total]
        (spread,) = totals
        spread = lax.all_to_all(spread, (*BLK, "feat"), 0, 0, tiled=True)
        scalar = ((1, 1), F32)
        big, small = hidden_weight.shape, (samples, points)
        outs = call(
            "update",
            update,
            [scalar, scalar]
            + [(big, F32)] * 3
            + [(big, BF)]
            + [(small, F32)] * 3
            + [(small, BF)],
            spread,
            mine,
            *grads,
            *alpha_grad,
            hidden_weight,
            hidden_moment,
            hidden_second,
            alpha,
            alpha_moment.T,
            alpha_second.T,
            last=True,
        )
        norm, resid = outs[:2]
        return (norm[0, 0], resid[0, 0], *outs[2:6], *[x.T for x in outs[6:]])

    return on_device


def solution(mesh):
    in_specs = (
        P(BLK, None),
        P(),
        P(BLK),
        P(BLK),
        P(None, "feat"),
        P("feat"),
        P(BLK),
        P(BLK, None),
        P(BLK, "feat"),
        P(BLK, "feat"),
        P(BLK, "feat"),
        P(BLK, None),
        P(BLK, None),
        P(BLK, None),
    )
    out_specs = (
        P(),
        P(),
        P(BLK, "feat"),
        P(BLK, "feat"),
        P(BLK, "feat"),
        P(BLK, "feat"),
        P(BLK, None),
        P(BLK, None),
        P(BLK, None),
        P(BLK, None),
    )
    n_blk, n_feat = mesh.shape["blk"], mesh.shape["feat"]
    inner = Mesh(mesh.devices.reshape(n_blk // 2, 2, n_feat), (*BLK, "feat"))
    on_device = build(n_blk, n_feat)
    return jax.shard_map(
        on_device, mesh=inner, in_specs=in_specs, out_specs=out_specs, check_vma=False
    )
```

```python
import jax
import jax.numpy as jnp
from jax import lax
from jax.experimental import pallas as pl
from jax.experimental.pallas import tpu as pltpu
from jax.sharding import Mesh
from jax.sharding import PartitionSpec as P

ADAM_STEP = 10
NOISE = 0.01
CLIP_AT = 0.01
BETA_ONE = 0.9
BETA_TWO = 0.999
ADAM_EPS = 1e-08
DECAY = 0.01
SHARES = (3, 5)
CHUNKS = len(SHARES)
TOGETHER = 1
LANES = 128
SCRATCH = 16 << 20
BIAS_A = 8_000_000_000
BF = jnp.bfloat16
F32 = jnp.float32
BLK = ("hi", "core")


def adamw_update(weight, moment, second, gradient, step_rate):
    moment = BETA_ONE * moment + (1.0 - BETA_ONE) * gradient
    second = BETA_TWO * second + (1.0 - BETA_TWO) * gradient * gradient
    moment_hat = moment / (1.0 - BETA_ONE**ADAM_STEP)
    second_hat = second / (1.0 - BETA_TWO**ADAM_STEP)
    weight = weight - step_rate * (moment_hat / (jnp.sqrt(second_hat) + ADAM_EPS) + DECAY * weight)
    return (weight, moment, second)


def swap(x, axis, size, mask):
    return lax.ppermute(x, axis, [(i, i ^ mask) for i in range(size)])


def dot(a, b, dims=((1,), (0,))):
    return lax.dot_general(a, b, (dims, ((), ())), preferred_element_type=F32)


def after(x, earlier):
    return lax.optimization_barrier((x, earlier))[0]


def split_low(x):
    high = x.astype(BF)
    return high, (x - high.astype(F32)).astype(BF)


def sine_cosine(x):
    turns = jnp.round(x * 0.6366197723675814)
    rest = x - turns * 1.5703125
    rest = rest - turns * 0.00048351287841796875
    rest = rest - turns * 3.1385570764541626e-07
    rest = rest - turns * 6.077100628276711e-11
    turns = turns.astype(jnp.int32)
    s = rest * rest
    sin_part = rest + rest * s * (-1.6666654611e-1 + s * (8.3321608736e-3 + s * (-1.9515295891e-4)))
    cos_part = 1.0 - 0.5 * s + s * s * (
        4.166664568298827e-2 + s * (-1.388731625493765e-3 + s * 2.443315711809948e-5)
    )
    even = (turns & 1) == 0
    sine = jnp.where(even, sin_part, cos_part)
    cosine = jnp.where(even, cos_part, sin_part)
    sine = jnp.where((turns & 2) == 0, sine, -sine)
    cosine = jnp.where(((turns + 1) & 2) == 0, cosine, -cosine)
    return sine, cosine


def groups_of(size):
    bits = [1 << k for k in range(1, size.bit_length() - 1)]
    if len(bits) < 2:
        return [bits]
    return [[bits[0], bits[1], bits[0] | bits[1]]] + [[b] for b in bits[2:]]


def call(name, body, outs, *args, last=False, weight=1):
    shapes = jax.ShapeDtypeStruct if last else pltpu.VMEM
    return pl.pallas_call(
        body,
        out_shape=[shapes(shape, dtype) for shape, dtype in outs],
        cost_estimate=pl.CostEstimate(flops=weight, transcendentals=0, bytes_accessed=1),
        compiler_params=pltpu.CompilerParams(vmem_limit_bytes=SCRATCH),
        name=name,
    )(*[pltpu.with_memory_space_constraint(x, pltpu.VMEM) for x in args])


def my_half():
    return lax.axis_index("feat")


def turned(x):
    own = x.shape[0] // 2
    core = lax.axis_index("core")
    low, high = x[:own], x[own:]
    return jnp.concatenate(
        [jnp.where(core == 0, low, high), jnp.where(core == 0, high, low)], axis=0
    )


def freq_rows(freq_ref, half, start, count):
    total = freq_ref.shape[0] // 2
    return freq_ref[pl.ds(pl.multiple_of(half * total + start, LANES), count), :]


def pieces_of(whole):
    ends = [whole * sum(SHARES[:k]) // sum(SHARES) for k in range(CHUNKS + 1)]
    return [slice(a, b) for a, b in zip(ends[:-1], ends[1:])]


def core_halves(mid):
    core = lax.axis_index("core")
    return [pl.ds(pl.multiple_of(k * mid, LANES), mid) for k in (core, 1 - core)]


def prepare(inputs, width_class, col_mask, masked):
    d_in = inputs.shape[1]
    n_blk = lax.axis_size("hi") * 2
    rows = d_in // n_blk
    classes = col_mask.shape[0]
    me = lax.axis_index("hi") * 2
    chosen = width_class[...] == lax.broadcasted_iota(jnp.int32, (classes, inputs.shape[0]), 0)
    keep_cols = dot(chosen.astype(F32), col_mask[...].astype(F32), ((0,), (0,)))
    plain = inputs[...] * keep_cols.astype(BF)
    tile = min(256, d_in)
    n_bits, shift = n_blk.bit_length() - 1, rows.bit_length() - 1
    for t in range(d_in // tile):
        column = lax.broadcasted_iota(jnp.int32, (1, tile), 1) + t * tile
        place = column >> shift
        source = jnp.zeros_like(place)
        for k in range(n_bits):
            source = source | (((place >> k) & 1) << (n_bits - 1 - k))
        source = ((source ^ me) << shift) | (column & (rows - 1))
        select = lax.broadcasted_iota(jnp.int32, (d_in, tile), 0) == source
        select = jnp.where(select, 1.0, 0.0).astype(BF)
        masked[:, t * tile : (t + 1) * tile] = dot(plain, select).astype(BF)


def hidden_units(masked, *refs):
    helds, (hidden, damp) = refs[: 1 if len(refs) == 3 else 2], refs[-2:]
    if len(helds) == 1:
        value = dot(masked[...], helds[0][...])
    else:
        parts = core_halves(masked.shape[1] // 2)
        value = sum(dot(masked[:, part], held[...]) for part, held in zip(parts, helds))
    value = jnp.tanh(value)
    hidden[...] = value.astype(BF)
    damp[...] = 1.0 - value * value


def first_pre(hidden, far, freq, phases, pre):
    width = hidden.shape[1]
    value = phases[...] + dot(hidden[...], freq_rows(freq, my_half(), 0, width))
    pre[...] = value + dot(far[...], freq_rows(freq, 1 - my_half(), 0, width))


def second_pre(pre, hidden, freq, out):
    width = hidden.shape[1]
    start = freq.shape[0] // 2 - width
    out[...] = pre[...] + dot(hidden[...], freq_rows(freq, my_half(), start, width))


def payload(keep, send, value, scalar):
    own = keep.shape[0]
    n_low = value.shape[1]
    keep[:, :n_low] = value[:own]
    keep[:, n_low:] = jnp.full((own, LANES), scalar, F32)
    send[:, :n_low] = value[own:]
    send[:, n_low:] = jnp.full((own, LANES), scalar, F32)


def make_features(pre, far, freq, alpha, row_mask, features, slope, keep, send):
    width = far.shape[1]
    scale = (2.0 / (pre.shape[1] * lax.axis_size("feat"))) ** 0.5
    start = freq.shape[0] // 2 - width
    angle = pre[...] + dot(far[...], freq_rows(freq, 1 - my_half(), start, width))
    sine, cosine = sine_cosine(angle)
    value = (scale * cosine).astype(BF)
    features[...] = value
    slope[...] = -scale * sine
    moments = dot(turned(alpha[...]).astype(BF), value)
    payload(keep, send, moments, jnp.sum(row_mask[...].astype(F32)))


def fit(mine, other, features, moments, fitted):
    n_low = features.shape[1]
    value = jnp.concatenate([mine[:, :n_low], other[:, :n_low]], axis=0)
    parts = jnp.concatenate(split_low(value), axis=0)
    moments[...] = parts
    both = dot(parts, features[...], ((1,), (1,)))
    samples = value.shape[0]
    fitted[...] = both[:samples] + both[samples:]


def residuals(near, far, mine, alpha, targets, prior, row_mask, features, resid_grad, keep, send):
    samples = alpha.shape[0]
    n_low = features.shape[1]
    true_count = jnp.maximum(mine[0:1, n_low : n_low + 1], 1.0)
    residual = near[...] + far[...] + NOISE * turned(alpha[...]) - targets[...] - turned(prior[...])
    keep_rows = row_mask[...].astype(F32)
    value = (2.0 * keep_rows * residual / (true_count * samples)).astype(BF)
    resid_grad[...] = value
    payload(keep, send, dot(value, features[...]), jnp.sum(keep_rows * residual * residual))


def pre_gradient(mine, other, moments, resid_grad, alpha, slope, freq, back, pre_grad, away):
    n_low = slope.shape[1]
    value = jnp.concatenate([mine[:, :n_low], other[:, :n_low]], axis=0)
    parts = jnp.concatenate(split_low(value), axis=0)
    back[...] = parts
    low = turned(alpha[...]).astype(BF)
    resid = resid_grad[...]
    left = jnp.concatenate([resid, resid, low, low], axis=0)
    right = jnp.concatenate([moments[...], parts], axis=0)
    grad = (slope[...] * dot(left, right, ((0,), (0,)))).astype(BF)
    pre_grad[...] = grad
    width = away.shape[1]
    start = freq.shape[0] // 2 - width
    away[...] = dot(grad, freq_rows(freq, 1 - my_half(), start, width), ((1,), (1,))).astype(BF)


def second_away(pre_grad, freq, away):
    width = away.shape[1]
    away[...] = dot(
        pre_grad[...], freq_rows(freq, 1 - my_half(), 0, width), ((1,), (1,))
    ).astype(BF)


def own_gradient(pre_grad, freq, back, features, near, pulled):
    near[...] = dot(pre_grad[...], freq_rows(freq, my_half(), 0, near.shape[1]), ((1,), (1,)))
    both = dot(back[...], features[...], ((1,), (1,)))
    samples = pulled.shape[0]
    pulled[...] = both[:samples] + both[samples:]


def weight_terms(part):
    def body(near, got, damp, masked, *refs):
        *pulls, send, keep = refs if len(refs) == 2 else refs[:-1]
        hidden_grad = near[:, part] + got[...].astype(F32)
        first_grad = (damp[...] * hidden_grad).astype(BF)
        mid = send.shape[0]
        own, other = core_halves(mid)
        send[...] = dot(masked[:, other], first_grad, ((0,), (0,))).astype(BF)
        keep[...] = dot(masked[:, own], first_grad, ((0,), (0,)))
        if pulls:
            pulled, pulled_far, resid_grad = pulls
            refs[-1][...] = pulled[...] + pulled_far[...] + NOISE * resid_grad[...].astype(F32)

    return body


def add_halves(keep, got, send, rest):
    mid = rest.shape[0]
    start = 0
    if got.shape[0] != keep.shape[0]:
        start = pl.multiple_of((1 - lax.axis_index("core")) * 2 * mid, mid)
    send[...] = (keep[mid:] + got[pl.ds(start + mid, mid)].astype(F32)).astype(BF)
    rest[...] = keep[:mid] + got[pl.ds(start, mid)].astype(F32)


def finish_gradients(keep, got, *refs):
    *earlier, weight_grad, total = refs
    value = keep[...] + got[...].astype(F32)
    weight_grad[...] = value
    whole = jnp.sum(value * value)
    if earlier:
        alpha_grad, before = earlier
        own = alpha_grad[...]
        whole = whole + before[0, 0] + jnp.where(my_half() == 0, jnp.sum(own * own), 0.0)
    total[...] = jnp.full(total.shape, whole, F32)


def update(*refs):
    spread, squares, *grads = refs[: 2 + CHUNKS]
    alpha_grad, *refs = refs[2 + CHUNKS :]
    weight, moment, second, alpha, alpha_moment, alpha_second = refs[:6]
    norm_out, resid_out = refs[6:8]
    norm = jnp.sqrt(jnp.sum(spread[:, :, 0:1], axis=0))
    norm_out[...] = norm
    last = squares.shape[1] - 1
    resid_out[...] = jnp.sqrt(squares[0:1, last:])
    clip = jnp.minimum(1.0, CLIP_AT / (norm + 1e-06))
    work = [
        (part, (weight, moment, second), grad[...], 0.02, refs[8:12])
        for part, grad in zip(pieces_of(weight.shape[1]), grads)
    ]
    held = (alpha, alpha_moment, alpha_second)
    work.append((slice(None), held, turned(alpha_grad[...]), 0.05, refs[12:16]))
    for part, values, grad, rate, outs in work:
        new = adamw_update(*[v[:, part] for v in values], grad * clip, rate)
        for out, value in zip(outs, (*new, new[0].astype(BF))):
            out[:, part] = value


def build(n_blk, n_feat):
    masks = [1 << k for k in range(n_blk.bit_length() - 1)]
    size = n_blk * n_feat

    def sum_over_blk(keep, send):
        keep = keep + swap(send, BLK, n_blk, 1)
        for group in groups_of(n_blk):
            keep = keep + sum(swap(keep, BLK, n_blk, m) for m in group)
        return keep, swap(keep, BLK, n_blk, 1)

    def on_device(
        inputs,
        col_mask,
        row_mask,
        width_class,
        frequencies,
        phases,
        targets,
        prior_draws,
        hidden_weight,
        hidden_moment,
        hidden_second,
        alpha_weight,
        alpha_moment,
        alpha_second,
    ):
        d_in = col_mask.shape[1]
        points, samples = alpha_weight.shape
        n_low = frequencies.shape[1]
        h_own = hidden_weight.shape[1]
        pieces = pieces_of(h_own)
        widths = [p.stop - p.start for p in pieces]
        row_mask, width_class, phases, targets = (
            x.reshape(1, -1) for x in (row_mask, width_class, phases, targets)
        )
        alpha, prior = alpha_weight.T, prior_draws.T

        low = hidden_weight.astype(BF)
        (masked,) = call(
            "prepare", prepare, [((points, d_in), BF)], inputs, width_class, col_mask
        )
        partly = []
        for c in range(CHUNKS):
            held = low[:, pieces[c]]
            for m in reversed(masks[1:]):
                held = jnp.concatenate([held, swap(held, BLK, n_blk, m)], axis=0)
            partly.append(held)
        units = [[((points, w), BF), ((points, w), F32)] for w in widths]
        wide = ((points, n_low), F32)
        held = lax.all_gather(partly[0], "core", axis=0, tiled=True)
        hidden, damp = call("hidden", hidden_units, units[0], masked, held)
        far = swap(hidden, "feat", n_feat, 1)
        (pre,) = call(
            "first_pre", first_pre, [wide], hidden, far, frequencies, phases, weight=BIAS_A
        )
        helds = [partly[1], swap(partly[1], BLK, n_blk, 1)]
        hidden, damp_b = call("hidden", hidden_units, units[1], masked, *helds, pre)
        damps = [damp, damp_b]
        far = swap(hidden, "feat", n_feat, 1)
        (pre,) = call("second_pre", second_pre, [wide], pre, hidden, frequencies)
        pair = [((samples // 2, n_low + LANES), F32)] * 2
        features, slope, keep, send = call(
            "features",
            make_features,
            [((points, n_low), BF), wide, *pair],
            pre,
            far,
            frequencies,
            alpha,
            row_mask,
        )
        mine, other = sum_over_blk(keep, send)
        parts = ((2 * samples, n_low), BF)
        thin = ((samples, points), F32)
        moments, fitted = call("fit", fit, [parts, thin], mine, other, features)
        fitted_far = swap(fitted, "feat", n_feat, 1)
        resid_grad, keep, send = call(
            "residuals",
            residuals,
            [((samples, points), BF), *pair],
            fitted,
            fitted_far,
            mine,
            alpha,
            targets,
            prior,
            row_mask,
            features,
        )
        mine, other = sum_over_blk(keep, send)
        away = [((points, width), BF) for width in widths]
        back, pre_grad, first = call(
            "pre_gradient",
            pre_gradient,
            [parts, ((points, n_low), BF), away[1]],
            mine,
            other,
            moments,
            resid_grad,
            alpha,
            slope,
            frequencies,
        )
        gots = [swap(first, "feat", n_feat, 1)]
        (second,) = call("second_away", second_away, away[:1], pre_grad, frequencies)
        gots.insert(0, swap(second, "feat", n_feat, 1))
        near, pulled = call(
            "own_gradient",
            own_gradient,
            [((points, h_own), F32), thin],
            pre_grad,
            frequencies,
            back,
            features,
        )
        pulled_far = swap(pulled, "feat", n_feat, 1)

        grads, totals = [], []
        for c in reversed(range(CHUNKS)):
            mid = d_in // 2
            width = widths[c]
            shapes = [((mid, width), BF), ((mid, width), F32)]
            operands = [near, gots[c], damps[c], masked]
            if c == 0:
                operands += [pulled, pulled_far, resid_grad]
                shapes = shapes + [thin]
            send, keep, *alpha_grad = call("weight_terms", weight_terms(pieces[c]), shapes, *operands)
            for m in masks[:-1]:
                if c < TOGETHER and m == masks[0]:
                    got = lax.all_gather(send, "core", axis=0, tiled=True)
                else:
                    got = swap(send, BLK, n_blk, m)
                mid = mid // 2
                shapes = [((mid, width), BF), ((mid, width), F32)]
                send, keep = call("add_halves", add_halves, shapes, keep, got)
            got = swap(send, BLK, n_blk, masks[-1])
            last = c == 0
            outs = [((mid, width), F32), ((size, 1, LANES) if last else (1, LANES), F32)]
            grad, total = call(
                "finish",
                finish_gradients,
                outs,
                keep,
                got,
                *alpha_grad,
                *totals,
            )
            grads.insert(0, grad)
            totals = [total]
        (spread,) = totals
        spread = lax.all_to_all(spread, (*BLK, "feat"), 0, 0, tiled=True)
        scalar = ((1, 1), F32)
        big, small = hidden_weight.shape, (samples, points)
        outs = call(
            "update",
            update,
            [scalar, scalar]
            + [(big, F32)] * 3
            + [(big, BF)]
            + [(small, F32)] * 3
            + [(small, BF)],
            spread,
            mine,
            *grads,
            *alpha_grad,
            hidden_weight,
            hidden_moment,
            hidden_second,
            alpha,
            alpha_moment.T,
            alpha_second.T,
            last=True,
        )
        norm, resid = outs[:2]
        return (norm[0, 0], resid[0, 0], *outs[2:6], *[x.T for x in outs[6:]])

    return on_device


def solution(mesh):
    in_specs = (
        P(BLK, None),
        P(),
        P(BLK),
        P(BLK),
        P(None, "feat"),
        P("feat"),
        P(BLK),
        P(BLK, None),
        P(BLK, "feat"),
        P(BLK, "feat"),
        P(BLK, "feat"),
        P(BLK, None),
        P(BLK, None),
        P(BLK, None),
    )
    out_specs = (
        P(),
        P(),
        P(BLK, "feat"),
        P(BLK, "feat"),
        P(BLK, "feat"),
        P(BLK, "feat"),
        P(BLK, None),
        P(BLK, None),
        P(BLK, None),
        P(BLK, None),
    )
    n_blk, n_feat = mesh.shape["blk"], mesh.shape["feat"]
    inner = Mesh(mesh.devices.reshape(n_blk // 2, 2, n_feat), (*BLK, "feat"))
    on_device = build(n_blk, n_feat)
    return jax.shard_map(
        on_device, mesh=inner, in_specs=in_specs, out_specs=out_specs, check_vma=False
    )
```
